32 devices in a mesh: groups: 2 (over y), width: 4 (over z), hidden: 2 (over x), batch: 2 (over core).
Axes of the slice: x: 2, y: 2, z: 4, core: 2. Of those that a mesh axis runs over, the one named last changes fastest.
Arguments:
- inputs: bfloat16 [2, 32, 16384], P(None, 'groups', 'width'), parts along dimension 1, may hold values from -42 to 42
- norm_gain: float32 [16384], P('width'), may hold values from 0.25 to 1.75
- wq_packed: int32 [16384, 4096], P('width', 'hidden'), may hold values from 0 to 255, as said below
- wq_scales: float32 [128, 8192], P('width', 'hidden'), may hold values from 0.002578125 to 0.01015625
- key_weight: bfloat16 [16384, 512], P('width', 'hidden'), may hold values from -0.046875 to 0.046875
- value_weight: bfloat16 [16384, 512], P('width', 'hidden'), may hold values from -0.046875 to 0.046875
- wo_weight: bfloat16 [8192, 16384], P('hidden', 'width'), may hold values from -0.3125 to 0.3125
- key_cache: bfloat16 [32, 1024, 512], P(('groups', 'width', 'batch'), None, 'hidden'), parts along dimension 0, may hold values from -6 to 6
- value_cache: bfloat16 [32, 1024, 512], P(('groups', 'width', 'batch'), None, 'hidden'), parts along dimension 0, may hold values from -6 to 6
- lengths: int32 [32], P(('groups', 'width', 'batch')), parts along dimension 0, may hold values from 256 to 1022, as said below
Outputs:
- attended: bfloat16 [2, 32, 16384], P(None, ('groups', 'hidden', 'batch'), 'width'), parts along dimension 1
The draws below stay inside these ranges and needn't reach their ends.
There are 2 independent parts, one for each index of `groups`. The reference program is written for one: setup_inputs(seed, part) draws one part's arguments, and reference() takes and returns one part's arrays. A program takes and returns all parts, laid end to end along the dimension named above; an argument that names none is the same for every part. Nothing has to cross between parts.
Inputs may be any that keep to these rules, and one draw needn't show every extreme that they name: `wq_packed`: each word holds two 4-bit codes, bits 4 c to 4 c + 3 for column 2 j + c. `lengths`: some sequence has exactly 1022 filled slots.
All inputs are finite; a program needn't handle non-finite values.
Results may differ from the reference program's by a relative error of at most 0.0091.
Values may be sent and summed in bfloat16 or wider, within the bound.
No kernel may reach another device: no remote copies, remote signals or barrier semaphores. Data moves between devices by JAX's collectives and lax.ppermute only.
A program may use at most 448 MiB of HBM per device.

```python
import math
import jax
import jax.numpy as jnp
from jax import lax

D = 16384
HEAD = 128
HQ = 64
KVH = 4
GROUP = 128
S = 1024
STEPS = 2
B = 16


def draw_inputs(key, part):
    key_base, key_cols = jax.random.split(key, 2)
    column = jnp.arange(D, dtype=jnp.float32) / D
    column_scale = jnp.exp(math.log(3.0) * column) * jnp.exp(jax.random.uniform(key_cols, (D,), jnp.float32, -0.7, 0.7))
    base = jnp.clip(jax.random.normal(key_base, (STEPS, B, D), jnp.float32), -4.0, 4.0)
    return (base * column_scale[None, None, :]).astype(jnp.bfloat16)


def draw_wq_packed(key, part):
    codes = jax.random.randint(key, (D, HQ * HEAD // 2, 2), 0, 16, dtype=jnp.int32)
    word = codes[..., 0] | codes[..., 1] << 4
    return word.at[0, 0].set(255).astype(jnp.int32)


def draw_lengths(key, part):
    key_len, key_pick = jax.random.split(key)
    filled = jax.random.randint(key_len, (B,), S // 4, S - 1, dtype=jnp.int32)
    chosen = jax.random.randint(key_pick, (), 0, B, dtype=jnp.int32)
    return jnp.where(jnp.arange(B, dtype=jnp.int32) == chosen, S - 2, filled).astype(jnp.int32)


def levels(stream_key, dims, cuts, least, largest):
    loudness, own = 1.0, jax.random.fold_in(stream_key, 6)
    for position, shards_of in cuts:
        draws = jnp.exp(jax.random.uniform(jax.random.fold_in(own, position), (shards_of,), jnp.float32, least / len(cuts), largest / len(cuts)))
        loudness = loudness * jnp.repeat(draws, dims[position] // shards_of).reshape([-1 if axis == position else 1 for axis in range(len(dims))])
    return loudness


def noise(key, dims, scale, most, pieces=(), kind=jnp.bfloat16):
    array = jax.random.normal(key, dims, jnp.float32) * scale
    if len(pieces) > 0:
        array = levels(key, dims, pieces, -0.22, 0.18) * array
    return jnp.clip(array, min=-most, max=most).astype(kind)


def setup_inputs(seed: int = 0, part: int = 0) -> dict:
    arg_keys = jax.random.split(jax.random.key(seed), 11)
    part_keys = jax.random.split(jax.random.fold_in(arg_keys[10], part), 11)
    return {
        "inputs": draw_inputs(jax.random.fold_in(jax.random.fold_in(arg_keys[10], part), 71), part),
        "norm_gain": jnp.clip(1.0 + 0.15 * jax.random.normal(arg_keys[1], (D,), jnp.float32), 0.25, 1.75),
        "wq_packed": draw_wq_packed(jax.random.fold_in(arg_keys[10], 71), part),
        "wq_scales": jnp.clip(jnp.exp(math.log(0.01015625) - 1.3710268 * jax.random.uniform(arg_keys[3], (D // GROUP, HQ * HEAD), jnp.float32) ** levels(arg_keys[3], (D // GROUP, HQ * HEAD), ((0, 4), (1, 2)), -0.2, 0.2)), 0.002578125, 0.01015625),
        "key_weight": noise(arg_keys[4], (D, KVH * HEAD), D ** -0.5, 0.046875, ((0, 4), (1, 2))),
        "value_weight": noise(arg_keys[5], (D, KVH * HEAD), D ** -0.5, 0.046875, ((0, 4), (1, 2))),
        "wo_weight": noise(arg_keys[6], (HQ * HEAD, D), (4.8 / (HQ * HEAD) ** 0.5), 0.3125, ((0, 2), (1, 4))),
        "key_cache": noise(part_keys[7], (B, S, KVH * HEAD), 1.0, 6.0, ((0, 8), (2, 2))),
        "value_cache": noise(part_keys[8], (B, S, KVH * HEAD), 1.0, 6.0, ((0, 8), (2, 2))),
        "lengths": draw_lengths(jax.random.fold_in(jax.random.fold_in(arg_keys[10], part), 71), part),
    }


def unpack_weights(packed, scales, bits, per_word):
    shifts = jnp.arange(per_word, dtype=jnp.int32) * bits
    codes = packed[:, :, None] >> shifts & (1 << bits) - 1
    values = (codes - (1 << bits - 1)).astype(jnp.float32)
    values = values.reshape(packed.shape[0], packed.shape[1] * per_word)
    group_rows = packed.shape[0] // scales.shape[0]
    values = values.reshape(scales.shape[0], group_rows, values.shape[1]) * scales[:, None, :]
    return values.reshape(packed.shape[0], -1)

def rotate_heads(field, positions):
    half = field.shape[-1] // 2
    freq = 500000.0 ** (-2.0 * jnp.arange(half, dtype=jnp.float32) / field.shape[-1])
    angle = positions.astype(jnp.float32)[:, None] * freq[None, :]
    cosine = jnp.cos(angle)[:, None, :]
    sine = jnp.sin(angle)[:, None, :]
    first = field[..., :half]
    second = field[..., half:]
    return jnp.concatenate([first * cosine - second * sine, second * cosine + first * sine], axis=-1)

def reference(inputs, norm_gain, wq_packed, wq_scales, key_weight, value_weight, wo_weight, key_cache, value_cache, lengths):
    high = lax.Precision.HIGHEST
    w_query = unpack_weights(wq_packed, wq_scales, 4, 2)
    w_output = wo_weight.astype(jnp.float32)
    w_key = key_weight.astype(jnp.float32)
    w_value = value_weight.astype(jnp.float32)
    seqs = lengths.shape[0]
    slots = key_cache.shape[1]
    repeat = HQ // KVH
    keys_all = key_cache
    values_all = value_cache
    results = []
    for step in range(STEPS):
        rows = inputs[step].astype(jnp.float32)
        scale = lax.rsqrt(lax.optimization_barrier(jnp.mean(rows * rows, axis=1, keepdims=True)) + 1e-05)
        normed = rows * scale * norm_gain[None, :]
        queries = jnp.dot(normed, w_query, precision=high, preferred_element_type=jnp.float32)
        keys_new = jnp.dot(normed, w_key, precision=high, preferred_element_type=jnp.float32)
        values_new = jnp.dot(normed, w_value, precision=high, preferred_element_type=jnp.float32)
        positions = lengths + step
        queries = rotate_heads(queries.reshape(seqs, HQ, HEAD), positions).astype(jnp.bfloat16)
        keys_new = rotate_heads(keys_new.reshape(seqs, KVH, HEAD), positions).reshape(seqs, KVH * HEAD).astype(jnp.bfloat16)
        values_new = values_new.astype(jnp.bfloat16)
        slot_ids = jnp.arange(slots, dtype=jnp.int32)
        written = slot_ids[None, :, None] == positions[:, None, None]
        keys_all = jnp.where(written, keys_new[:, None, :], keys_all)
        values_all = jnp.where(written, values_new[:, None, :], values_all)
        query_heads = queries.reshape(seqs, KVH, repeat, HEAD).astype(jnp.float32)
        key_heads = keys_all.reshape(seqs, slots, KVH, HEAD).astype(jnp.float32)
        value_heads = values_all.reshape(seqs, slots, KVH, HEAD).astype(jnp.float32)
        scores = jnp.einsum('bgrd,bsgd->bgrs', query_heads, key_heads) * HEAD ** (-0.5)
        valid = slot_ids[None, None, None, :] <= positions[:, None, None, None]
        scores = jnp.where(valid, scores, -1e+30)
        peak = lax.optimization_barrier(jnp.max(scores, axis=-1, keepdims=True))
        weights = jnp.exp(scores - peak)
        total = lax.optimization_barrier(jnp.sum(weights, axis=-1, keepdims=True))
        probs = (weights / total).astype(jnp.bfloat16)
        mixed = jnp.einsum('bgrs,bsgd->bgrd', probs.astype(jnp.float32), value_heads)
        mixed = mixed.reshape(seqs, HQ * HEAD).astype(jnp.bfloat16)
        attended = jnp.dot(mixed.astype(jnp.float32), w_output, precision=high, preferred_element_type=jnp.float32)
        results.append(attended.astype(jnp.bfloat16))
    return jnp.stack(results)
```

```python
import jax
import jax.numpy as jnp
from jax import lax
from jax.experimental import pallas as pl
from jax.experimental.pallas import tpu as pltpu
from jax.sharding import PartitionSpec as P

D = 16384
HEAD = 128
STEPS = 2
EPS = 1e-05
BF16 = jnp.bfloat16
F32 = jnp.float32
VMEM_LIMIT = 60 * 1024 * 1024


def unpack_weights(packed, scales, bits, per_word):
    shifts = jnp.arange(per_word, dtype=jnp.int32) * bits
    codes = packed[:, :, None] >> shifts & (1 << bits) - 1
    values = (codes - (1 << bits - 1)).astype(jnp.float32)
    values = values.reshape(packed.shape[0], packed.shape[1] * per_word)
    group_rows = packed.shape[0] // scales.shape[0]
    values = values.reshape(scales.shape[0], group_rows, values.shape[1]) * scales[:, None, :]
    return values.reshape(packed.shape[0], -1)


def rotate_heads(field, positions):
    half = field.shape[-1] // 2
    freq = 500000.0 ** (-2.0 * jnp.arange(half, dtype=jnp.float32) / field.shape[-1])
    angle = positions.astype(jnp.float32)[:, None] * freq[None, :]
    cosine = jnp.cos(angle)[:, None, :]
    sine = jnp.sin(angle)[:, None, :]
    first = field[..., :half]
    second = field[..., half:]
    return jnp.concatenate(
        [first * cosine - second * sine, second * cosine + first * sine], axis=-1
    )


def general(
    inputs,
    norm_gain,
    wq_packed,
    wq_scales,
    key_weight,
    value_weight,
    wo_weight,
    key_cache,
    value_cache,
    lengths,
):
    high = lax.Precision.HIGHEST
    w_query = unpack_weights(wq_packed, wq_scales, 4, 2)
    w_output = wo_weight.astype(jnp.float32)
    w_joined = jnp.concatenate(
        [w_query, key_weight.astype(jnp.float32), value_weight.astype(jnp.float32)], axis=1
    )
    seq_local = lengths.shape[0]
    slots = key_cache.shape[1]
    kv_local = key_weight.shape[1] // HEAD
    q_local = w_query.shape[1] // HEAD
    repeat = q_local // kv_local
    cols_local = inputs.shape[2]
    keys_all = key_cache
    values_all = value_cache
    slot_ids = jnp.arange(slots, dtype=jnp.int32)
    results = []
    for step in range(STEPS):
        rows = inputs[step].astype(jnp.float32)
        width_count = lax.axis_size("width")
        batch_count = lax.axis_size("batch")
        arranged = rows.reshape(width_count, batch_count, seq_local, cols_local)
        rows = lax.dynamic_index_in_dim(arranged, lax.axis_index("batch"), 1, keepdims=False)
        rows = rows.reshape(width_count * seq_local, cols_local)
        squares = jnp.sum(rows * rows, axis=1)
        total = lax.psum(squares, "width")
        scale = lax.rsqrt(total / D + EPS)
        normed = rows * scale[:, None] * norm_gain[None, :]
        partial_value = jnp.dot(
            normed, w_joined, precision=high, preferred_element_type=jnp.float32
        )
        projected = lax.psum_scatter(partial_value, "width", scatter_dimension=0, tiled=True)
        positions = lengths + step
        q_cols = q_local * HEAD
        kv_cols = kv_local * HEAD
        queries = rotate_heads(
            projected[:, :q_cols].reshape(seq_local, q_local, HEAD), positions
        ).astype(jnp.bfloat16)
        keys_new = rotate_heads(
            projected[:, q_cols : q_cols + kv_cols].reshape(seq_local, kv_local, HEAD), positions
        )
        keys_new = keys_new.reshape(seq_local, kv_cols).astype(jnp.bfloat16)
        values_new = projected[:, q_cols + kv_cols :].astype(jnp.bfloat16)
        written = slot_ids[None, :, None] == positions[:, None, None]
        keys_all = jnp.where(written, keys_new[:, None, :], keys_all)
        values_all = jnp.where(written, values_new[:, None, :], values_all)
        query_heads = queries.reshape(seq_local, kv_local, repeat, HEAD)
        key_heads = keys_all.reshape(seq_local, slots, kv_local, HEAD)
        value_heads = values_all.reshape(seq_local, slots, kv_local, HEAD)
        scores = jnp.einsum(
            "bgrd,bsgd->bgrs", query_heads, key_heads, preferred_element_type=jnp.float32
        ) * HEAD ** (-0.5)
        valid = slot_ids[None, None, None, :] <= positions[:, None, None, None]
        scores = jnp.where(valid, scores, -1e30)
        peak = jnp.max(scores, axis=-1, keepdims=True)
        weights = jnp.exp(scores - peak)
        total_weight = jnp.sum(weights, axis=-1, keepdims=True)
        probs = (weights / total_weight).astype(jnp.bfloat16)
        mixed = jnp.einsum(
            "bgrs,bsgd->bgrd", probs, value_heads, preferred_element_type=jnp.float32
        )
        mixed = mixed.reshape(seq_local, q_cols).astype(jnp.bfloat16)
        out_terms = jnp.dot(
            lax.all_gather(mixed, ("width", "batch"), axis=0, tiled=True).astype(jnp.float32),
            w_output,
            precision=high,
            preferred_element_type=jnp.float32,
        )
        head_sums = lax.psum_scatter(out_terms, "hidden", scatter_dimension=0, tiled=True)
        share = head_sums.shape[0] // lax.axis_size("batch")
        attended = lax.dynamic_slice_in_dim(head_sums, lax.axis_index("batch") * share, share, 0)
        results.append(attended.astype(jnp.bfloat16))
    return jnp.stack(results)


def split3(value):
    hi = value.astype(BF16)
    rest = value - hi.astype(F32)
    mid = rest.astype(BF16)
    low = (rest - mid.astype(F32)).astype(BF16)
    return hi, mid, low


def project_kernel(
    x_ref, gain_ref, wq_ref, scale_ref, kw_ref, vw_ref, own_ref, *rest
):
    nw = len(rest) - 5
    sends = rest[: nw - 1]
    se_ref, so_ref, acc_ref, ss_ref, kv_ref, arr_ref = rest[nw - 1 :]
    k = pl.program_id(0)
    steps, seqs, depth = x_ref.shape
    rows = steps * seqs
    words = wq_ref.shape[1]
    groups = se_ref.shape[0]
    per_block = groups // pl.num_programs(0)
    group = depth // per_block

    @pl.when(k == 0)
    def _():
        acc_ref[...] = jnp.zeros_like(acc_ref)
        ss_ref[...] = jnp.zeros_like(ss_ref)
        kv_ref[...] = jnp.zeros_like(kv_ref)
        row = lax.broadcasted_iota(jnp.int32, (256, 256), 0)
        col = lax.broadcasted_iota(jnp.int32, (256, 256), 1)
        pick = jnp.where(row == 2 * (col & 127) + (col >> 7), 1.0, 0.0).astype(BF16)
        for c in range(words // 128):
            terms = split3(scale_ref[:, c * 256 : (c + 1) * 256])
            parts = [jnp.dot(term, pick, preferred_element_type=F32) for term in terms]
            both = parts[0] + (parts[1] + parts[2])
            se_ref[:, c * 128 : (c + 1) * 128] = both[:, :128]
            so_ref[:, c * 128 : (c + 1) * 128] = both[:, 128:]

    x = x_ref[...].astype(F32).reshape(rows, depth)
    y = x * gain_ref[...]
    hi = y.astype(BF16)
    low = (y - hi.astype(F32)).astype(BF16)
    lhs = jnp.concatenate([hi, low], axis=0)
    exact = hi.astype(F32) + low.astype(F32)
    sums = [
        8.0 * jnp.sum(exact[:, g * group : (g + 1) * group], axis=1, keepdims=True)
        for g in range(per_block)
    ]
    squares = x * x
    total = squares[:, :128]
    for c in range(1, depth // 128):
        total = total + squares[:, c * 128 : (c + 1) * 128]
    ss_ref[...] += total

    chunk = 256
    for c in range(words // chunk):
        cols = slice(c * chunk, (c + 1) * chunk)
        even = jnp.zeros((rows, chunk), F32)
        odd = jnp.zeros((rows, chunk), F32)
        for g in range(per_block):
            span = slice(g * group, (g + 1) * group)
            word = wq_ref[span, cols]
            both = word.astype(F32).astype(BF16)
            upper = (word >> 4).astype(F32).astype(BF16)
            left = lhs[:, span]
            p = jnp.dot(left, both, preferred_element_type=F32)
            u = jnp.dot(left, upper, preferred_element_type=F32)
            p = p[:rows] + p[rows:]
            u = u[:rows] + u[rows:]
            at = pl.ds(k * per_block + g, 1)
            even = even + (p - 16.0 * u - sums[g]) * se_ref[at, cols]
            odd = odd + (u - sums[g]) * so_ref[at, cols]
        acc_ref[:, cols] += even
        acc_ref[:, words + c * chunk : words + (c + 1) * chunk] += odd
    key = jnp.dot(lhs, kw_ref[...], preferred_element_type=F32)
    val = jnp.dot(lhs, vw_ref[...], preferred_element_type=F32)
    kv_ref[:, :HEAD] += key[:rows] + key[rows:]
    kv_ref[:, HEAD:] += val[:rows] + val[rows:]

    @pl.when(k == pl.num_programs(0) - 1)
    def _():
        each = seqs // nw
        lane = lax.broadcasted_iota(jnp.int32, (rows, 128), 1)
        a, m, l = split3(jnp.sum(ss_ref[...], axis=1, keepdims=True))
        a, m, l = a.astype(F32), m.astype(F32), l.astype(F32)
        norm = jnp.where(lane == 0, a, jnp.where(lane == 1, m, jnp.where(lane == 2, l, 0.0)))
        for v in range(nw):
            for t in range(steps):
                src = slice(t * seqs + v * each, t * seqs + (v + 1) * each)
                dst = slice(t * each, (t + 1) * each)
                arr_ref[v, dst, : 2 * words] = acc_ref[src, :]
                arr_ref[v, dst, 2 * words : 2 * words + 2 * HEAD] = kv_ref[src, :]
                arr_ref[v, dst, 2 * words + 2 * HEAD :] = norm[src]
        me = lax.axis_index("width")
        own_ref[...] = arr_ref[me]
        for s in range(1, nw):
            sends[s - 1][...] = arr_ref[lax.rem(me + s, nw)].astype(BF16)


def project(inputs, norm_gain, wq_packed, wq_scales, key_weight, value_weight, nw, nb):
    steps, seqs, depth = inputs.shape
    rows = steps * seqs
    words = wq_packed.shape[1] // nb
    groups = wq_scales.shape[0]
    block = 512
    cols = 2 * words + 3 * HEAD
    out_rows = rows // nw
    mine = lambda k: (k, lax.axis_index("batch"))
    return pl.pallas_call(
        project_kernel,
        grid=(depth // block,),
        in_specs=[
            pl.BlockSpec((steps, seqs, block), lambda k: (0, 0, k)),
            pl.BlockSpec((1, block), lambda k: (0, k)),
            pl.BlockSpec((block, words), mine),
            pl.BlockSpec((groups, 2 * words), lambda k: (0, lax.axis_index("batch"))),
            pl.BlockSpec((block, HEAD), mine),
            pl.BlockSpec((block, HEAD), mine),
        ],
        out_specs=[pl.BlockSpec((out_rows, cols), lambda k: (0, 0))] * nw,
        out_shape=[jax.ShapeDtypeStruct((out_rows, cols), F32)]
        + [jax.ShapeDtypeStruct((out_rows, cols), BF16)] * (nw - 1),
        scratch_shapes=[
            pltpu.VMEM((groups, words), F32),
            pltpu.VMEM((groups, words), F32),
            pltpu.VMEM((rows, 2 * words), F32),
            pltpu.VMEM((rows, 128), F32),
            pltpu.VMEM((rows, 2 * HEAD), F32),
            pltpu.VMEM((nw, out_rows, cols), F32),
        ],
        compiler_params=pltpu.CompilerParams(vmem_limit_bytes=VMEM_LIMIT),
        name="project",
    )(inputs, norm_gain.reshape(1, -1), wq_packed, wq_scales, key_weight, value_weight)


def attend_kernel(heads, nw, len_ref, own_ref, *rest):
    parts = rest[: nw - 1]
    (table_ref, k_own, k_mate, v_own, v_mate, out_ref, k_buf, v_buf, q_ref, m_ref, sems) = rest[nw - 1 :]
    each, slots, _ = k_own.shape
    b = lax.axis_index("batch")
    column = pl.ds(pl.multiple_of(b * HEAD, HEAD), HEAD)
    copies = []
    for n, (src, buf, place) in enumerate(
        ((k_own, k_buf, b), (k_mate, k_buf, 1 - b), (v_own, v_buf, b), (v_mate, v_buf, 1 - b))
    ):
        copy = pltpu.make_async_copy(
            src.at[:, :, column], buf.at[pl.ds(place * each, each)], sems.at[n]
        )
        copy.start()
        copies.append(copy)

    rows = own_ref.shape[0]
    seqs = rows // STEPS
    half = heads * HEAD // 2
    total = own_ref[...]
    for part in parts:
        total = total + part[...].astype(F32)
    squares = jnp.sum(total[:, 2 * half + 2 * HEAD :], axis=1, keepdims=True)
    total = total * lax.rsqrt(squares / D + EPS)

    lane = lax.broadcasted_iota(jnp.int32, (rows, HEAD), 1)
    left = lane < HEAD // 2
    tiles = []
    for m in range(heads // 2):
        e = total[:, m * HEAD : (m + 1) * HEAD]
        o = total[:, half + m * HEAD : half + (m + 1) * HEAD]
        tiles.append(jnp.where(left, e, pltpu.roll(o, HEAD // 2, 1)))
        tiles.append(jnp.where(left, pltpu.roll(e, HEAD // 2, 1), o))
    cos_q, sin_q = table_ref[0], table_ref[1]
    cos_k, sin_k = table_ref[2], table_ref[3]
    near = (lane & (HEAD // 2 - 1)) < HEAD // 4
    turned = []
    for q in tiles:
        other = jnp.where(near, pltpu.roll(q, HEAD - HEAD // 4, 1), pltpu.roll(q, HEAD // 4, 1))
        turned.append(q * cos_q + other * sin_q)
    q_all = jnp.concatenate(turned, axis=0).astype(BF16)
    row = lax.broadcasted_iota(jnp.int32, (HEAD, HEAD), 0)
    col = lax.broadcasted_iota(jnp.int32, (HEAD, HEAD), 1)
    order = jnp.where(col == 2 * (row & (HEAD // 2 - 1)) + row // (HEAD // 2), 1.0, 0.0).astype(BF16)
    q_ref[...] = jnp.dot(q_all, order, preferred_element_type=F32)
    k_new = total[:, 2 * half : 2 * half + HEAD]
    k_new = (k_new * cos_k + pltpu.roll(k_new, HEAD // 2, 1) * sin_k).astype(BF16).astype(F32)
    v_new = total[:, 2 * half + HEAD : 2 * half + 2 * HEAD].astype(BF16).astype(F32)

    for copy in copies:
        copy.wait()

    slot = lax.broadcasted_iota(jnp.int32, (STEPS * heads, slots), 1)
    later = lax.broadcasted_iota(jnp.int32, (STEPS * heads, 1), 0) >= heads
    for j in range(seqs):
        q = jnp.concatenate(
            [q_ref[pl.ds(t * seqs + j, heads, stride=rows), :] for t in range(STEPS)], axis=0
        )
        scores = lax.dot_general(
            q.astype(BF16), k_buf[j], (((1,), (1,)), ((), ())), preferred_element_type=F32
        ) * HEAD ** (-0.5)
        scores = jnp.where(slot < len_ref[j], scores, -1e30)
        first = jnp.sum(q * k_new[j : j + 1], axis=1, keepdims=True) * HEAD ** (-0.5)
        second = jnp.sum(q * k_new[seqs + j : seqs + j + 1], axis=1, keepdims=True) * HEAD ** (-0.5)
        second = jnp.where(later, second, -1e30)
        peak = jnp.maximum(jnp.max(scores, axis=1, keepdims=True), jnp.maximum(first, second))
        weights = jnp.exp(scores - peak)
        first = jnp.exp(first - peak)
        second = jnp.exp(second - peak)
        inverse = 1.0 / (jnp.sum(weights, axis=1, keepdims=True) + first + second)
        probs = (weights * inverse).astype(BF16)
        mixed = jnp.dot(probs, v_buf[j], preferred_element_type=F32)
        mixed = mixed + (first * inverse).astype(BF16).astype(F32) * v_new[j : j + 1]
        mixed = mixed + (second * inverse).astype(BF16).astype(F32) * v_new[seqs + j : seqs + j + 1]
        for t in range(STEPS):
            m_ref[pl.ds(t * seqs + j, heads, stride=rows), :] = mixed[t * heads : (t + 1) * heads]
    for n in range(heads):
        out_ref[:, n * HEAD : (n + 1) * HEAD] = m_ref[n * rows : (n + 1) * rows, :].astype(BF16)


def attend(own, parts, table, lengths, k_own, k_mate, v_own, v_mate, heads):
    rows = own.shape[0]
    each, slots, _ = k_own.shape
    nw = len(parts) + 1
    vmem = pl.BlockSpec(memory_space=pltpu.VMEM)
    hbm = pl.BlockSpec(memory_space=pl.ANY)
    body = lambda *refs: attend_kernel(heads, nw, *refs)
    return pl.pallas_call(
        body,
        in_specs=[pl.BlockSpec(memory_space=pltpu.SMEM)] + [vmem] * (nw + 1) + [hbm] * 4,
        out_specs=vmem,
        out_shape=jax.ShapeDtypeStruct((rows, heads * HEAD), BF16),
        scratch_shapes=[
            pltpu.VMEM((2 * each, slots, HEAD), BF16),
            pltpu.VMEM((2 * each, slots, HEAD), BF16),
            pltpu.VMEM((heads * rows, HEAD), F32),
            pltpu.VMEM((heads * rows, HEAD), F32),
            pltpu.SemaphoreType.DMA((4,)),
        ],
        compiler_params=pltpu.CompilerParams(vmem_limit_bytes=VMEM_LIMIT),
        name="attend",
    )(lengths, own, *parts, table, k_own, k_mate, v_own, v_mate)


def output_kernel(nw, *refs):
    pieces = refs[:nw]
    wo_ref = refs[nw]
    outs = refs[nw + 1 : 2 * nw + 1]
    lhs_ref, acc_ref = refs[2 * nw + 1 :]
    rows, depth = pieces[0].shape

    @pl.when(pl.program_id(0) == 0)
    def _():
        me = lax.axis_index("width")
        for s in range(nw):
            lhs_ref[lax.rem(me + nw - s, nw)] = pieces[s][...].astype(F32)

    lhs = lhs_ref[...].reshape(nw * rows, depth).astype(BF16)
    acc = jnp.dot(lhs, wo_ref[...], preferred_element_type=F32)
    acc_ref[...] = acc.reshape(acc_ref.shape)
    me = lax.axis_index("hidden") * lax.axis_size("batch") + lax.axis_index("batch")
    outs[0][...] = acc_ref[me]
    for s in range(1, nw):
        outs[s][...] = acc_ref[me ^ s].astype(BF16)


def output(pieces, wo_weight):
    nw = len(pieces)
    rows, depth = pieces[0].shape
    cols = wo_weight.shape[1]
    block = 512
    body = lambda *refs: output_kernel(nw, *refs)
    return pl.pallas_call(
        body,
        grid=(cols // block,),
        in_specs=[pl.BlockSpec((rows, depth), lambda n: (0, 0))] * nw
        + [pl.BlockSpec((depth, block), lambda n: (lax.axis_index("batch"), n))],
        out_specs=[pl.BlockSpec((rows, block), lambda n: (0, n))] * nw,
        out_shape=[jax.ShapeDtypeStruct((rows, cols), F32)]
        + [jax.ShapeDtypeStruct((rows, cols), BF16)] * (nw - 1),
        scratch_shapes=[
            pltpu.VMEM((nw, rows, depth), F32),
            pltpu.VMEM((nw, rows, block), F32),
        ],
        compiler_params=pltpu.CompilerParams(vmem_limit_bytes=VMEM_LIMIT),
        name="output",
    )(*pieces, wo_weight)


def rotary_tables(positions):
    lane = jnp.arange(HEAD, dtype=jnp.int32)
    parity = 2 * (lane % (HEAD // 2)) + lane // (HEAD // 2)
    out = []
    for dim in (parity, lane):
        pair = (dim % (HEAD // 2)).astype(F32)
        freq = 500000.0 ** (-2.0 * pair / HEAD)
        angle = positions.astype(F32)[:, None] * freq[None, :]
        sign = jnp.where(dim < HEAD // 2, -1.0, 1.0)[None, :]
        out += [jnp.cos(angle), jnp.sin(angle) * sign]
    return jnp.stack(out)


def split_heads(
    inputs,
    norm_gain,
    wq_packed,
    wq_scales,
    key_weight,
    value_weight,
    wo_weight,
    key_cache,
    value_cache,
    lengths,
):
    nw, nh, nb = lax.axis_size("width"), lax.axis_size("hidden"), lax.axis_size("batch")
    swap = [(0, 1), (1, 0)]
    k_mate = lax.ppermute(key_cache, "batch", swap)
    v_mate = lax.ppermute(value_cache, "batch", swap)
    len_mate = lax.ppermute(lengths, "batch", swap)
    first = lax.axis_index("batch") == 0
    len_all = jnp.where(
        first, jnp.concatenate([lengths, len_mate]), jnp.concatenate([len_mate, lengths])
    )
    positions = jnp.concatenate([len_all + step for step in range(STEPS)])
    table = rotary_tables(positions)

    own, *sends = project(
        inputs, norm_gain, wq_packed, wq_scales, key_weight, value_weight, nw, nb
    )
    parts = [
        lax.ppermute(piece, "width", [(i, (i + s) % nw) for i in range(nw)])
        for s, piece in enumerate(sends, 1)
    ]
    heads = 2 * wq_packed.shape[1] // nb // HEAD
    mixed = attend(own, parts, table, len_all, key_cache, k_mate, value_cache, v_mate, heads)
    pieces = [mixed] + [
        lax.ppermute(mixed, "width", [(i, (i + s) % nw) for i in range(nw)]) for s in range(1, nw)
    ]
    head_own, *head_sends = output(pieces, wo_weight)
    sums = head_own
    for s, piece in enumerate(head_sends, 1):
        got = lax.ppermute(piece, ("hidden", "batch"), [(i, i ^ s) for i in range(nh * nb)])
        sums = sums + got.astype(F32)
    return sums.reshape(STEPS, -1, sums.shape[1]).astype(BF16)


def solution(mesh):
    sizes = mesh.shape

    def on_device(*args):
        kv_local = args[4].shape[1] // HEAD
        fits = (
            sizes["batch"] == 2
            and kv_local == 2
            and sizes["width"] == sizes["hidden"] * sizes["batch"]
            and args[0].shape[1] // sizes["width"] == 2 * args[9].shape[0]
            and args[0].shape[2] % 512 == 0
            and STEPS * args[0].shape[1] // sizes["width"] % 8 == 0
        )
        return split_heads(*args) if fits else general(*args)

    in_specs = (
        P(None, "groups", "width"),
        P("width"),
        P("width", "hidden"),
        P("width", "hidden"),
        P("width", "hidden"),
        P("width", "hidden"),
        P("hidden", "width"),
        P(("groups", "width", "batch"), None, "hidden"),
        P(("groups", "width", "batch"), None, "hidden"),
        P(("groups", "width", "batch")),
    )
    out_specs = P(None, ("groups", "hidden", "batch"), "width")
    return jax.shard_map(
        on_device, mesh=mesh, in_specs=in_specs, out_specs=out_specs, check_vma=False
    )
```

```python
import jax
import jax.numpy as jnp
from jax import lax
from jax.experimental import pallas as pl
from jax.experimental.pallas import tpu as pltpu
from jax.sharding import PartitionSpec as P

D = 16384
HEAD = 128
STEPS = 2
EPS = 1e-05
BF16 = jnp.bfloat16
F32 = jnp.float32
MIB = 1024 * 1024
PROJECT_LIMIT = 26 * MIB
ATTEND_LIMIT = 10 * MIB
OUTPUT_LIMIT = 10 * MIB
FETCH_LIMIT = 1 * MIB
HBM = pl.BlockSpec(memory_space=pltpu.HBM)
ANY = pl.BlockSpec(memory_space=pl.ANY)
VMEM = pl.BlockSpec(memory_space=pltpu.VMEM)


def unpack_weights(packed, scales, bits, per_word):
    shifts = jnp.arange(per_word, dtype=jnp.int32) * bits
    codes = packed[:, :, None] >> shifts & (1 << bits) - 1
    values = (codes - (1 << bits - 1)).astype(jnp.float32)
    values = values.reshape(packed.shape[0], packed.shape[1] * per_word)
    group_rows = packed.shape[0] // scales.shape[0]
    values = values.reshape(scales.shape[0], group_rows, values.shape[1]) * scales[:, None, :]
    return values.reshape(packed.shape[0], -1)


def rotate_heads(field, positions):
    half = field.shape[-1] // 2
    freq = 500000.0 ** (-2.0 * jnp.arange(half, dtype=jnp.float32) / field.shape[-1])
    angle = positions.astype(jnp.float32)[:, None] * freq[None, :]
    cosine = jnp.cos(angle)[:, None, :]
    sine = jnp.sin(angle)[:, None, :]
    first = field[..., :half]
    second = field[..., half:]
    return jnp.concatenate(
        [first * cosine - second * sine, second * cosine + first * sine], axis=-1
    )


def general(
    inputs,
    norm_gain,
    wq_packed,
    wq_scales,
    key_weight,
    value_weight,
    wo_weight,
    key_cache,
    value_cache,
    lengths,
):
    high = lax.Precision.HIGHEST
    w_query = unpack_weights(wq_packed, wq_scales, 4, 2)
    w_output = wo_weight.astype(jnp.float32)
    w_joined = jnp.concatenate(
        [w_query, key_weight.astype(jnp.float32), value_weight.astype(jnp.float32)], axis=1
    )
    seq_local = lengths.shape[0]
    slots = key_cache.shape[1]
    kv_local = key_weight.shape[1] // HEAD
    q_local = w_query.shape[1] // HEAD
    repeat = q_local // kv_local
    cols_local = inputs.shape[2]
    keys_all = key_cache
    values_all = value_cache
    slot_ids = jnp.arange(slots, dtype=jnp.int32)
    results = []
    for step in range(STEPS):
        rows = inputs[step].astype(jnp.float32)
        width_count = lax.axis_size("width")
        batch_count = lax.axis_size("batch")
        arranged = rows.reshape(width_count, batch_count, seq_local, cols_local)
        rows = lax.dynamic_index_in_dim(arranged, lax.axis_index("batch"), 1, keepdims=False)
        rows = rows.reshape(width_count * seq_local, cols_local)
        squares = jnp.sum(rows * rows, axis=1)
        total = lax.psum(squares, "width")
        scale = lax.rsqrt(total / D + EPS)
        normed = rows * scale[:, None] * norm_gain[None, :]
        partial_value = jnp.dot(
            normed, w_joined, precision=high, preferred_element_type=jnp.float32
        )
        projected = lax.psum_scatter(partial_value, "width", scatter_dimension=0, tiled=True)
        positions = lengths + step
        q_cols = q_local * HEAD
        kv_cols = kv_local * HEAD
        queries = rotate_heads(
            projected[:, :q_cols].reshape(seq_local, q_local, HEAD), positions
        ).astype(jnp.bfloat16)
        keys_new = rotate_heads(
            projected[:, q_cols : q_cols + kv_cols].reshape(seq_local, kv_local, HEAD), positions
        )
        keys_new = keys_new.reshape(seq_local, kv_cols).astype(jnp.bfloat16)
        values_new = projected[:, q_cols + kv_cols :].astype(jnp.bfloat16)
        written = slot_ids[None, :, None] == positions[:, None, None]
        keys_all = jnp.where(written, keys_new[:, None, :], keys_all)
        values_all = jnp.where(written, values_new[:, None, :], values_all)
        query_heads = queries.reshape(seq_local, kv_local, repeat, HEAD)
        key_heads = keys_all.reshape(seq_local, slots, kv_local, HEAD)
        value_heads = values_all.reshape(seq_local, slots, kv_local, HEAD)
        scores = jnp.einsum(
            "bgrd,bsgd->bgrs", query_heads, key_heads, preferred_element_type=jnp.float32
        ) * HEAD ** (-0.5)
        valid = slot_ids[None, None, None, :] <= positions[:, None, None, None]
        scores = jnp.where(valid, scores, -1e30)
        peak = jnp.max(scores, axis=-1, keepdims=True)
        weights = jnp.exp(scores - peak)
        total_weight = jnp.sum(weights, axis=-1, keepdims=True)
        probs = (weights / total_weight).astype(jnp.bfloat16)
        mixed = jnp.einsum(
            "bgrs,bsgd->bgrd", probs, value_heads, preferred_element_type=jnp.float32
        )
        mixed = mixed.reshape(seq_local, q_cols).astype(jnp.bfloat16)
        out_terms = jnp.dot(
            lax.all_gather(mixed, ("width", "batch"), axis=0, tiled=True).astype(jnp.float32),
            w_output,
            precision=high,
            preferred_element_type=jnp.float32,
        )
        head_sums = lax.psum_scatter(out_terms, "hidden", scatter_dimension=0, tiled=True)
        share = head_sums.shape[0] // lax.axis_size("batch")
        attended = lax.dynamic_slice_in_dim(head_sums, lax.axis_index("batch") * share, share, 0)
        results.append(attended.astype(jnp.bfloat16))
    return jnp.stack(results)


def split3(value):
    hi = value.astype(BF16)
    rest = value - hi.astype(F32)
    mid = rest.astype(BF16)
    low = (rest - mid.astype(F32)).astype(BF16)
    return hi, mid, low


def project_kernel(
    x_hbm, gain_hbm, wq_hbm, scale_hbm, kw_hbm, vw_hbm, own_ref, *rest
):
    nw = len(rest) - 11
    sends = rest[: nw - 1]
    (
        x_ref, gain_ref, wq_ref, scale_ref, kv_ref, se_ref, so_ref, y_ref, acc_ref, ss_ref, sems,
        block_sems,
    ) = rest[nw - 1 :]
    steps, seqs, depth = x_ref.shape
    rows = steps * seqs
    each = seqs // nw
    blocks, block, words = wq_ref.shape
    groups = se_ref.shape[0]
    per_block = groups // blocks
    group = block // per_block
    b = lax.axis_index("batch")

    def columns(n):
        return pl.ds(pl.multiple_of(b * n, n), n)

    def fetch(i):
        return pltpu.make_async_copy(
            wq_hbm.at[pl.ds(pl.multiple_of(i * block, block), block), columns(words)],
            wq_ref.at[i],
            block_sems.at[i],
        )

    scale_copy = pltpu.make_async_copy(scale_hbm.at[:, columns(2 * words)], scale_ref, sems.at[0])
    others = [
        pltpu.make_async_copy(gain_hbm, gain_ref, sems.at[1]),
        pltpu.make_async_copy(x_hbm, x_ref, sems.at[4]),
    ]
    kvs = [
        pltpu.make_async_copy(kw_hbm.at[:, columns(HEAD)], kv_ref.at[:, :HEAD], sems.at[2]),
        pltpu.make_async_copy(vw_hbm.at[:, columns(HEAD)], kv_ref.at[:, HEAD:], sems.at[3]),
    ]
    scale_copy.start()
    for copy in others:
        copy.start()
    for i in range(4):
        fetch(i).start()

    acc_ref[...] = jnp.zeros_like(acc_ref)
    ss_ref[...] = jnp.zeros_like(ss_ref)
    row = lax.broadcasted_iota(jnp.int32, (256, 256), 0)
    col = lax.broadcasted_iota(jnp.int32, (256, 256), 1)
    pick = jnp.where(row == 2 * (col & 127) + (col >> 7), 1.0, 0.0).astype(BF16)
    scale_copy.wait()
    for c in range(words // 128):
        terms = split3(scale_ref[:, c * 256 : (c + 1) * 256])
        parts = [jnp.dot(term, pick, preferred_element_type=F32) for term in terms]
        both = parts[0] + (parts[1] + parts[2])
        se_ref[:, c * 128 : (c + 1) * 128] = both[:, :128]
        so_ref[:, c * 128 : (c + 1) * 128] = both[:, 128:]
    for copy in others:
        copy.wait()

    chunk = 256

    def step(i, carry):
        here = pl.ds(pl.multiple_of(i * block, block), block)
        x = x_ref[:, :, here].astype(F32)
        x = jnp.concatenate(
            [x[t, v * each : (v + 1) * each] for v in range(nw) for t in range(steps)], axis=0
        )
        y = x * gain_ref[:, here]
        hi = y.astype(BF16)
        low = (y - hi.astype(F32)).astype(BF16)
        lhs = jnp.concatenate([hi, low], axis=0)
        y_ref[i] = lhs
        squares = x * x
        ss_ref[...] += sum(squares[:, c * 128 : (c + 1) * 128] for c in range(block // 128))
        sums = [
            8.0 * jnp.sum(y[:, g * group : (g + 1) * group], axis=1, keepdims=True)
            for g in range(per_block)
        ]
        fetch(i).wait()

        @pl.when(i + 4 < blocks)
        def _():
            fetch(i + 4).start()

        @pl.when(i == 1)
        def _():
            for copy in kvs:
                copy.start()

        for c in range(words // chunk):
            cols = slice(c * chunk, (c + 1) * chunk)
            even = jnp.zeros((rows, chunk), F32)
            odd = jnp.zeros((rows, chunk), F32)
            for g in range(per_block):
                span = slice(g * group, (g + 1) * group)
                word = wq_ref[i, span, cols]
                both = word.astype(F32).astype(BF16)
                upper = (word >> 4).astype(F32).astype(BF16)
                left = lhs[:, span]
                p = jnp.dot(left, both, preferred_element_type=F32)
                u = jnp.dot(left, upper, preferred_element_type=F32)
                p = p[:rows] + p[rows:]
                u = u[:rows] + u[rows:]
                at = pl.ds(i * per_block + g, 1)
                even = even + (p - 16.0 * u - sums[g]) * se_ref[at, cols]
                odd = odd + (u - sums[g]) * so_ref[at, cols]
            acc_ref[:, cols] += even
            acc_ref[:, words + c * chunk : words + (c + 1) * chunk] += odd
        return carry

    def step_kv(i, carry):
        step(i, carry)
        new = jnp.zeros((2 * rows, 2 * HEAD), F32)
        for n in range(2):
            j = 2 * i - blocks + n
            at = pl.ds(pl.multiple_of(j * block, block), block)
            new = new + jnp.dot(y_ref[j], kv_ref[at], preferred_element_type=F32)
        acc_ref[:, 2 * words : 2 * words + 2 * HEAD] += new[:rows] + new[rows:]
        return carry

    lax.fori_loop(0, blocks // 2, step, 0, unroll=2)
    for copy in kvs:
        copy.wait()
    lax.fori_loop(blocks // 2, blocks - 1, step_kv, 0)
    step_kv(blocks - 1, 0)
    lane = lax.broadcasted_iota(jnp.int32, (rows, 128), 1)
    a, m, l = split3(jnp.sum(ss_ref[...], axis=1, keepdims=True))
    a, m, l = a.astype(F32), m.astype(F32), l.astype(F32)
    acc_ref[:, 2 * words + 2 * HEAD :] = jnp.where(
        lane == 0, a, jnp.where(lane == 1, m, jnp.where(lane == 2, l, 0.0))
    )

    me = lax.axis_index("width")
    share = rows // nw

    def piece(s):
        return acc_ref[pl.ds(pl.multiple_of(lax.rem(me + s, nw) * share, share), share)]

    own_ref[...] = piece(0)
    for s in range(1, nw):
        sends[s - 1][...] = piece(s).astype(BF16)


def in_hbm(array):
    return pltpu.with_memory_space_constraint(array, pltpu.HBM)


def project(inputs, norm_gain, wq_packed, wq_scales, key_weight, value_weight, nw, nb):
    steps, seqs, depth = inputs.shape
    rows = steps * seqs
    words = wq_packed.shape[1] // nb
    groups = wq_scales.shape[0]
    block = 256
    blocks = depth // block
    cols = 2 * words + 3 * HEAD
    out_rows = rows // nw
    return pl.pallas_call(
        project_kernel,
        in_specs=[HBM] * 6,
        out_specs=[VMEM] * nw,
        out_shape=[jax.ShapeDtypeStruct((out_rows, cols), F32)]
        + [jax.ShapeDtypeStruct((out_rows, cols), BF16)] * (nw - 1),
        scratch_shapes=[
            pltpu.VMEM((steps, seqs, depth), BF16),
            pltpu.VMEM((1, depth), F32),
            pltpu.VMEM((blocks, block, words), jnp.int32),
            pltpu.VMEM((groups, 2 * words), F32),
            pltpu.VMEM((depth, 2 * HEAD), BF16),
            pltpu.VMEM((groups, words), F32),
            pltpu.VMEM((groups, words), F32),
            pltpu.VMEM((blocks, 2 * rows, block), BF16),
            pltpu.VMEM((rows, cols), F32),
            pltpu.VMEM((rows, 128), F32),
            pltpu.SemaphoreType.DMA((5,)),
            pltpu.SemaphoreType.DMA((blocks,)),
        ],
        compiler_params=pltpu.CompilerParams(vmem_limit_bytes=PROJECT_LIMIT),
        name="project",
    )(
        *map(
            in_hbm,
            (inputs, norm_gain.reshape(1, -1), wq_packed, wq_scales, key_weight, value_weight),
        )
    )


def weight_copies(src, dst, start, depth, sems):
    first = lax.axis_index("batch") * depth + start
    count = sems.shape[0]
    each = dst.shape[0] // count
    return [
        pltpu.make_async_copy(
            src.at[pl.ds(pl.multiple_of(first + n * each, each), each)],
            dst.at[pl.ds(n * each, each)],
            sems.at[n],
        )
        for n in range(count)
    ]


def fetch_weight(wo_weight, start, size, depth, after):
    def body(src, after, dst, sems):
        del after
        copies = weight_copies(src, dst, start, depth, sems)
        for copy in copies:
            copy.start()
        for copy in copies:
            copy.wait()

    return pl.pallas_call(
        body,
        in_specs=[HBM, ANY],
        out_specs=VMEM,
        out_shape=pltpu.VMEM((size, wo_weight.shape[1]), BF16),
        scratch_shapes=[pltpu.SemaphoreType.DMA((size // 256,))],
        compiler_params=pltpu.CompilerParams(vmem_limit_bytes=FETCH_LIMIT),
        name="fetch",
    )(in_hbm(wo_weight), after)


def attend_kernel(heads, nw, start, len_ref, own_ref, *rest):
    parts = rest[: nw - 1]
    (
        table_ref, k_own, k_mate, v_own, v_mate, wo_hbm, _, out_ref, wo_ref, k_buf, v_buf, q_ref,
        m_ref, sems, wo_sems,
    ) = rest[nw - 1 :]
    each, slots, _ = k_own.shape
    b = lax.axis_index("batch")
    column = pl.ds(pl.multiple_of(b * HEAD, HEAD), HEAD)
    copies = [
        pltpu.make_async_copy(
            src.at[:, :, column], buf.at[pl.ds(place * each, each)], sems.at[n]
        )
        for n, (src, buf, place) in enumerate(
            ((k_own, k_buf, b), (k_mate, k_buf, 1 - b), (v_own, v_buf, b), (v_mate, v_buf, 1 - b))
        )
    ]
    incoming = weight_copies(wo_hbm, wo_ref, start, heads * HEAD, wo_sems)
    for copy in copies + incoming:
        copy.start()

    rows = own_ref.shape[0]
    seqs = rows // STEPS
    half = heads * HEAD // 2
    total = own_ref[...]
    for part in parts:
        total = total + part[...].astype(F32)
    squares = jnp.sum(total[:, 2 * half + 2 * HEAD :], axis=1, keepdims=True)
    total = total * lax.rsqrt(squares / D + EPS)

    lane = lax.broadcasted_iota(jnp.int32, (rows, HEAD), 1)
    left = lane < HEAD // 2
    tiles = []
    for m in range(heads // 2):
        e = total[:, m * HEAD : (m + 1) * HEAD]
        o = total[:, half + m * HEAD : half + (m + 1) * HEAD]
        tiles.append(jnp.where(left, e, pltpu.roll(o, HEAD // 2, 1)))
        tiles.append(jnp.where(left, pltpu.roll(e, HEAD // 2, 1), o))
    cos_q, sin_q = table_ref[0], table_ref[1]
    cos_k, sin_k = table_ref[2], table_ref[3]
    near = (lane & (HEAD // 2 - 1)) < HEAD // 4
    turned = []
    for q in tiles:
        other = jnp.where(near, pltpu.roll(q, HEAD - HEAD // 4, 1), pltpu.roll(q, HEAD // 4, 1))
        turned.append(q * cos_q + other * sin_q)
    q_all = jnp.concatenate(turned, axis=0).astype(BF16)
    row = lax.broadcasted_iota(jnp.int32, (HEAD, HEAD), 0)
    col = lax.broadcasted_iota(jnp.int32, (HEAD, HEAD), 1)
    order = jnp.where(col == 2 * (row & (HEAD // 2 - 1)) + row // (HEAD // 2), 1.0, 0.0).astype(BF16)
    q_ref[...] = jnp.dot(q_all, order, preferred_element_type=F32)
    k_new = total[:, 2 * half : 2 * half + HEAD]
    k_new = (k_new * cos_k + pltpu.roll(k_new, HEAD // 2, 1) * sin_k).astype(BF16).astype(F32)
    v_new = total[:, 2 * half + HEAD : 2 * half + 2 * HEAD].astype(BF16).astype(F32)

    for copy in copies:
        copy.wait()

    slot = lax.broadcasted_iota(jnp.int32, (STEPS * heads, slots), 1)
    later = lax.broadcasted_iota(jnp.int32, (STEPS * heads, 1), 0) >= heads
    for j in range(seqs):
        q = jnp.concatenate(
            [q_ref[pl.ds(t * seqs + j, heads, stride=rows), :] for t in range(STEPS)], axis=0
        )
        scores = lax.dot_general(
            q.astype(BF16), k_buf[j], (((1,), (1,)), ((), ())), preferred_element_type=F32
        ) * HEAD ** (-0.5)
        scores = jnp.where(slot < len_ref[j], scores, -1e30)
        first = jnp.sum(q * k_new[j : j + 1], axis=1, keepdims=True) * HEAD ** (-0.5)
        second = jnp.sum(q * k_new[seqs + j : seqs + j + 1], axis=1, keepdims=True) * HEAD ** (-0.5)
        second = jnp.where(later, second, -1e30)
        peak = jnp.maximum(jnp.max(scores, axis=1, keepdims=True), jnp.maximum(first, second))
        weights = jnp.exp(scores - peak)
        first = jnp.exp(first - peak)
        second = jnp.exp(second - peak)
        inverse = 1.0 / (jnp.sum(weights, axis=1, keepdims=True) + first + second)
        probs = (weights * inverse).astype(BF16)
        mixed = jnp.dot(probs, v_buf[j], preferred_element_type=F32)
        mixed = mixed + (first * inverse).astype(BF16).astype(F32) * v_new[j : j + 1]
        mixed = mixed + (second * inverse).astype(BF16).astype(F32) * v_new[seqs + j : seqs + j + 1]
        for t in range(STEPS):
            m_ref[pl.ds(t * seqs + j, heads, stride=rows), :] = mixed[t * heads : (t + 1) * heads]
    for n in range(heads):
        out_ref[:, n * HEAD : (n + 1) * HEAD] = m_ref[n * rows : (n + 1) * rows, :].astype(BF16)
    for copy in incoming:
        copy.wait()


def attend(own, parts, table, lengths, k_own, k_mate, v_own, v_mate, wo_weight, start, size, after, heads):
    rows = own.shape[0]
    each, slots, _ = k_own.shape
    nw = len(parts) + 1
    body = lambda *refs: attend_kernel(heads, nw, start, *refs)
    return pl.pallas_call(
        body,
        in_specs=[pl.BlockSpec(memory_space=pltpu.SMEM)] + [VMEM] * (nw + 1) + [ANY] * 4 + [HBM, ANY],
        out_specs=[VMEM, VMEM],
        out_shape=[
            jax.ShapeDtypeStruct((rows, heads * HEAD), BF16),
            pltpu.VMEM((size, wo_weight.shape[1]), BF16),
        ],
        scratch_shapes=[
            pltpu.VMEM((2 * each, slots, HEAD), BF16),
            pltpu.VMEM((2 * each, slots, HEAD), BF16),
            pltpu.VMEM((heads * rows, HEAD), F32),
            pltpu.VMEM((heads * rows, HEAD), F32),
            pltpu.SemaphoreType.DMA((4,)),
            pltpu.SemaphoreType.DMA((size // 256,)),
        ],
        compiler_params=pltpu.CompilerParams(vmem_limit_bytes=ATTEND_LIMIT),

        name="attend",
    )(lengths, own, *parts, table, in_hbm(k_own), k_mate, in_hbm(v_own), v_mate, in_hbm(wo_weight), after)


def output_kernel(nw, count, *refs):
    pieces = refs[:nw]
    weights = refs[nw : nw + count]
    outs = refs[nw + count : 2 * nw + count]
    piece_ref, acc_ref = refs[2 * nw + count :]
    rows, depth = pieces[0].shape
    cols = weights[0].shape[1]
    place = lax.axis_index("width")
    for s in range(nw):
        piece_ref[lax.rem(place + nw - s, nw)] = pieces[s][...].astype(F32)
    lhs = piece_ref[...].reshape(nw * rows, depth).astype(BF16)
    block = 512
    for n in range(cols // block):
        span = slice(n * block, (n + 1) * block)
        acc = jnp.zeros((nw * rows, block), F32)
        first = 0
        for w_ref in weights:
            last = first + w_ref.shape[0]
            acc = acc + jnp.dot(lhs[:, first:last], w_ref[:, span], preferred_element_type=F32)
            first = last
        acc_ref[:, :, span] = acc.reshape(nw, rows, block)
    me = lax.axis_index("hidden") * lax.axis_size("batch") + lax.axis_index("batch")
    for s in range(nw):
        value = acc_ref[me ^ s].astype(outs[s].dtype)
        for t in range(STEPS):
            outs[s][t] = value[t * rows // STEPS : (t + 1) * rows // STEPS]


def output(pieces, weights):
    nw, count = len(pieces), len(weights)
    rows, depth = pieces[0].shape
    cols = weights[0].shape[1]
    body = lambda *refs: output_kernel(nw, count, *refs)
    shape = (STEPS, rows // STEPS, cols)
    return pl.pallas_call(
        body,
        in_specs=[VMEM] * (nw + count),
        out_specs=[VMEM] * nw,
        out_shape=[jax.ShapeDtypeStruct(shape, F32)]
        + [jax.ShapeDtypeStruct(shape, BF16)] * (nw - 1),
        scratch_shapes=[
            pltpu.VMEM((nw, rows, depth), F32),
            pltpu.VMEM((nw, rows, cols), F32),
        ],
        compiler_params=pltpu.CompilerParams(vmem_limit_bytes=OUTPUT_LIMIT),
        name="output",
    )(*pieces, *weights)


def rotary_tables(positions):
    lane = jnp.arange(HEAD, dtype=jnp.int32)
    parity = 2 * (lane % (HEAD // 2)) + lane // (HEAD // 2)
    out = []
    for dim in (parity, lane):
        pair = (dim % (HEAD // 2)).astype(F32)
        freq = 500000.0 ** (-2.0 * pair / HEAD)
        angle = positions.astype(F32)[:, None] * freq[None, :]
        sign = jnp.where(dim < HEAD // 2, -1.0, 1.0)[None, :]
        out += [jnp.cos(angle), jnp.sin(angle) * sign]
    return jnp.stack(out)


def split_heads(
    inputs,
    norm_gain,
    wq_packed,
    wq_scales,
    key_weight,
    value_weight,
    wo_weight,
    key_cache,
    value_cache,
    lengths,
):
    nw, nh, nb = lax.axis_size("width"), lax.axis_size("hidden"), lax.axis_size("batch")
    swap = [(0, 1), (1, 0)]
    k_mate = lax.ppermute(key_cache, "batch", swap)
    v_mate = lax.ppermute(value_cache, "batch", swap)
    len_mate = lax.ppermute(lengths, "batch", swap)
    first = lax.axis_index("batch") == 0
    len_all = jnp.where(
        first, jnp.concatenate([lengths, len_mate]), jnp.concatenate([len_mate, lengths])
    )
    positions = jnp.concatenate([len_all + step for step in range(STEPS)])
    table = rotary_tables(positions)

    own, *sends = project(
        inputs, norm_gain, wq_packed, wq_scales, key_weight, value_weight, nw, nb
    )
    own, k_mate, v_mate, *sends = lax.optimization_barrier((own, k_mate, v_mate, *sends))
    parts = [
        lax.ppermute(piece, "width", [(i, (i + s) % nw) for i in range(nw)])
        for s, piece in enumerate(sends, 1)
    ]
    heads = 2 * wq_packed.shape[1] // nb // HEAD
    depth = heads * HEAD
    early, late = depth // 4, depth // 4
    middle = depth - early - late
    w_early = fetch_weight(wo_weight, 0, early, depth, own)
    mixed, w_middle = attend(
        own, parts, table, len_all, key_cache, k_mate, value_cache, v_mate, wo_weight, early, middle,
        w_early, heads,
    )
    w_late = fetch_weight(wo_weight, early + middle, late, depth, mixed)
    pieces = [mixed] + [
        lax.ppermute(mixed, "width", [(i, (i + s) % nw) for i in range(nw)]) for s in range(1, nw)
    ]
    head_own, *head_sends = output(pieces, [w_early, w_middle, w_late])
    sums = head_own
    for s, piece in enumerate(head_sends, 1):
        got = lax.ppermute(piece, ("hidden", "batch"), [(i, i ^ s) for i in range(nh * nb)])
        sums = sums + got.astype(F32)
    return sums.astype(BF16)


def solution(mesh):
    sizes = mesh.shape

    def on_device(*args):
        kv_local = args[4].shape[1] // HEAD
        fits = (
            sizes["batch"] == 2
            and kv_local == 2
            and sizes["width"] == sizes["hidden"] * sizes["batch"]
            and args[0].shape[1] // sizes["width"] == 2 * args[9].shape[0]
            and args[0].shape[2] % 512 == 0
            and STEPS * args[0].shape[1] // sizes["width"] % 8 == 0
        )
        return split_heads(*args) if fits else general(*args)

    in_specs = (
        P(None, "groups", "width"),
        P("width"),
        P("width", "hidden"),
        P("width", "hidden"),
        P("width", "hidden"),
        P("width", "hidden"),
        P("hidden", "width"),
        P(("groups", "width", "batch"), None, "hidden"),
        P(("groups", "width", "batch"), None, "hidden"),
        P(("groups", "width", "batch")),
    )
    out_specs = P(None, ("groups", "hidden", "batch"), "width")
    return jax.shard_map(
        on_device, mesh=mesh, in_specs=in_specs, out_specs=out_specs, check_vma=False
    )
```

```python
import jax
import jax.numpy as jnp
from jax import lax
from jax.experimental import pallas as pl
from jax.experimental.pallas import tpu as pltpu
from jax.sharding import PartitionSpec as P

D = 16384
HEAD = 128
STEPS = 2
EPS = 1e-05
BF16 = jnp.bfloat16
F32 = jnp.float32
MIB = 1024 * 1024
PROJECT_LIMIT = 26 * MIB
ATTEND_LIMIT = 10 * MIB
OUTPUT_LIMIT = 10 * MIB
FETCH_LIMIT = 1 * MIB
EARLY, MIDDLE, LATE = 2, 3, 3
HBM = pl.BlockSpec(memory_space=pltpu.HBM)
ANY = pl.BlockSpec(memory_space=pl.ANY)
VMEM = pl.BlockSpec(memory_space=pltpu.VMEM)


def unpack_weights(packed, scales, bits, per_word):
    shifts = jnp.arange(per_word, dtype=jnp.int32) * bits
    codes = packed[:, :, None] >> shifts & (1 << bits) - 1
    values = (codes - (1 << bits - 1)).astype(jnp.float32)
    values = values.reshape(packed.shape[0], packed.shape[1] * per_word)
    group_rows = packed.shape[0] // scales.shape[0]
    values = values.reshape(scales.shape[0], group_rows, values.shape[1]) * scales[:, None, :]
    return values.reshape(packed.shape[0], -1)


def rotate_heads(field, positions):
    half = field.shape[-1] // 2
    freq = 500000.0 ** (-2.0 * jnp.arange(half, dtype=jnp.float32) / field.shape[-1])
    angle = positions.astype(jnp.float32)[:, None] * freq[None, :]
    cosine = jnp.cos(angle)[:, None, :]
    sine = jnp.sin(angle)[:, None, :]
    first = field[..., :half]
    second = field[..., half:]
    return jnp.concatenate(
        [first * cosine - second * sine, second * cosine + first * sine], axis=-1
    )


def general(
    inputs,
    norm_gain,
    wq_packed,
    wq_scales,
    key_weight,
    value_weight,
    wo_weight,
    key_cache,
    value_cache,
    lengths,
):
    high = lax.Precision.HIGHEST
    w_query = unpack_weights(wq_packed, wq_scales, 4, 2)
    w_output = wo_weight.astype(jnp.float32)
    w_joined = jnp.concatenate(
        [w_query, key_weight.astype(jnp.float32), value_weight.astype(jnp.float32)], axis=1
    )
    seq_local = lengths.shape[0]
    slots = key_cache.shape[1]
    kv_local = key_weight.shape[1] // HEAD
    q_local = w_query.shape[1] // HEAD
    repeat = q_local // kv_local
    cols_local = inputs.shape[2]
    keys_all = key_cache
    values_all = value_cache
    slot_ids = jnp.arange(slots, dtype=jnp.int32)
    results = []
    for step in range(STEPS):
        rows = inputs[step].astype(jnp.float32)
        width_count = lax.axis_size("width")
        batch_count = lax.axis_size("batch")
        arranged = rows.reshape(width_count, batch_count, seq_local, cols_local)
        rows = lax.dynamic_index_in_dim(arranged, lax.axis_index("batch"), 1, keepdims=False)
        rows = rows.reshape(width_count * seq_local, cols_local)
        squares = jnp.sum(rows * rows, axis=1)
        total = lax.psum(squares, "width")
        scale = lax.rsqrt(total / D + EPS)
        normed = rows * scale[:, None] * norm_gain[None, :]
        partial_value = jnp.dot(
            normed, w_joined, precision=high, preferred_element_type=jnp.float32
        )
        projected = lax.psum_scatter(partial_value, "width", scatter_dimension=0, tiled=True)
        positions = lengths + step
        q_cols = q_local * HEAD
        kv_cols = kv_local * HEAD
        queries = rotate_heads(
            projected[:, :q_cols].reshape(seq_local, q_local, HEAD), positions
        ).astype(jnp.bfloat16)
        keys_new = rotate_heads(
            projected[:, q_cols : q_cols + kv_cols].reshape(seq_local, kv_local, HEAD), positions
        )
        keys_new = keys_new.reshape(seq_local, kv_cols).astype(jnp.bfloat16)
        values_new = projected[:, q_cols + kv_cols :].astype(jnp.bfloat16)
        written = slot_ids[None, :, None] == positions[:, None, None]
        keys_all = jnp.where(written, keys_new[:, None, :], keys_all)
        values_all = jnp.where(written, values_new[:, None, :], values_all)
        query_heads = queries.reshape(seq_local, kv_local, repeat, HEAD)
        key_heads = keys_all.reshape(seq_local, slots, kv_local, HEAD)
        value_heads = values_all.reshape(seq_local, slots, kv_local, HEAD)
        scores = jnp.einsum(
            "bgrd,bsgd->bgrs", query_heads, key_heads, preferred_element_type=jnp.float32
        ) * HEAD ** (-0.5)
        valid = slot_ids[None, None, None, :] <= positions[:, None, None, None]
        scores = jnp.where(valid, scores, -1e30)
        peak = jnp.max(scores, axis=-1, keepdims=True)
        weights = jnp.exp(scores - peak)
        total_weight = jnp.sum(weights, axis=-1, keepdims=True)
        probs = (weights / total_weight).astype(jnp.bfloat16)
        mixed = jnp.einsum(
            "bgrs,bsgd->bgrd", probs, value_heads, preferred_element_type=jnp.float32
        )
        mixed = mixed.reshape(seq_local, q_cols).astype(jnp.bfloat16)
        out_terms = jnp.dot(
            lax.all_gather(mixed, ("width", "batch"), axis=0, tiled=True).astype(jnp.float32),
            w_output,
            precision=high,
            preferred_element_type=jnp.float32,
        )
        head_sums = lax.psum_scatter(out_terms, "hidden", scatter_dimension=0, tiled=True)
        share = head_sums.shape[0] // lax.axis_size("batch")
        attended = lax.dynamic_slice_in_dim(head_sums, lax.axis_index("batch") * share, share, 0)
        results.append(attended.astype(jnp.bfloat16))
    return jnp.stack(results)


def split3(value):
    hi = value.astype(BF16)
    rest = value - hi.astype(F32)
    mid = rest.astype(BF16)
    low = (rest - mid.astype(F32)).astype(BF16)
    return hi, mid, low


def project_kernel(
    x_hbm, gain_hbm, wq_hbm, scale_hbm, kw_hbm, vw_hbm, own_ref, *rest
):
    nw = len(rest) - 11
    sends = rest[: nw - 1]
    (
        x_ref, gain_ref, wq_ref, scale_ref, kv_ref, se_ref, so_ref, y_ref, acc_ref, ss_ref, sems,
        block_sems,
    ) = rest[nw - 1 :]
    steps, seqs, depth = x_ref.shape
    rows = steps * seqs
    each = seqs // nw
    blocks, block, words = wq_ref.shape
    groups = se_ref.shape[0]
    per_block = groups // blocks
    group = block // per_block
    b = lax.axis_index("batch")

    def columns(n):
        return pl.ds(pl.multiple_of(b * n, n), n)

    def fetch(i):
        return pltpu.make_async_copy(
            wq_hbm.at[pl.ds(pl.multiple_of(i * block, block), block), columns(words)],
            wq_ref.at[i],
            block_sems.at[i],
        )

    scale_copy = pltpu.make_async_copy(scale_hbm.at[:, columns(2 * words)], scale_ref, sems.at[0])
    others = [
        pltpu.make_async_copy(gain_hbm, gain_ref, sems.at[1]),
        pltpu.make_async_copy(x_hbm, x_ref, sems.at[4]),
    ]
    kvs = [
        pltpu.make_async_copy(kw_hbm.at[:, columns(HEAD)], kv_ref.at[:, :HEAD], sems.at[2]),
        pltpu.make_async_copy(vw_hbm.at[:, columns(HEAD)], kv_ref.at[:, HEAD:], sems.at[3]),
    ]
    scale_copy.start()
    for copy in others:
        copy.start()
    for i in range(3):
        fetch(i).start()

    acc_ref[...] = jnp.zeros_like(acc_ref)
    ss_ref[...] = jnp.zeros_like(ss_ref)
    row = lax.broadcasted_iota(jnp.int32, (256, 256), 0)
    col = lax.broadcasted_iota(jnp.int32, (256, 256), 1)
    pick = jnp.where(row == 2 * (col & 127) + (col >> 7), 1.0, 0.0).astype(BF16)
    scale_copy.wait()
    for c in range(words // 128):
        terms = split3(scale_ref[:, c * 256 : (c + 1) * 256])
        parts = [jnp.dot(term, pick, preferred_element_type=F32) for term in terms]
        both = parts[0] + (parts[1] + parts[2])
        se_ref[:, c * 128 : (c + 1) * 128] = both[:, :128]
        so_ref[:, c * 128 : (c + 1) * 128] = both[:, 128:]
    for copy in others:
        copy.wait()

    chunk = 512

    def step(i, carry):
        here = pl.ds(pl.multiple_of(i * block, block), block)
        x = x_ref[:, :, here].astype(F32)
        x = jnp.concatenate(
            [x[t, v * each : (v + 1) * each] for v in range(nw) for t in range(steps)], axis=0
        )
        y = x * gain_ref[:, here]
        hi = y.astype(BF16)
        low = (y - hi.astype(F32)).astype(BF16)
        lhs = jnp.concatenate([hi, low], axis=0)
        y_ref[i] = lhs
        squares = x * x
        ss_ref[...] += sum(squares[:, c * 128 : (c + 1) * 128] for c in range(block // 128))
        sums = [
            8.0 * jnp.sum(y[:, g * group : (g + 1) * group], axis=1, keepdims=True)
            for g in range(per_block)
        ]
        fetch(i).wait()

        @pl.when(i + 3 < blocks)
        def _():
            fetch(i + 3).start()

        @pl.when(i == 0)
        def _():
            for copy in kvs:
                copy.start()

        for c in range(words // chunk):
            cols = slice(c * chunk, (c + 1) * chunk)
            even = jnp.zeros((rows, chunk), F32)
            odd = jnp.zeros((rows, chunk), F32)
            for g in range(per_block):
                span = slice(g * group, (g + 1) * group)
                word = wq_ref[i, span, cols]
                both = word.astype(F32).astype(BF16)
                upper = (word >> 4).astype(F32).astype(BF16)
                left = lhs[:, span]
                p = jnp.dot(left, both, preferred_element_type=F32)
                u = jnp.dot(left, upper, preferred_element_type=F32)
                p = p[:rows] + p[rows:]
                u = u[:rows] + u[rows:]
                at = pl.ds(i * per_block + g, 1)
                even = even + (p - 16.0 * u - sums[g]) * se_ref[at, cols]
                odd = odd + (u - sums[g]) * so_ref[at, cols]
            acc_ref[:, cols] += even
            acc_ref[:, words + c * chunk : words + (c + 1) * chunk] += odd
        return carry

    def step_kv(i, carry):
        step(i, carry)
        new = jnp.zeros((2 * rows, 2 * HEAD), F32)
        for n in range(2):
            j = 2 * i - blocks + n
            at = pl.ds(pl.multiple_of(j * block, block), block)
            new = new + jnp.dot(y_ref[j], kv_ref[at], preferred_element_type=F32)
        acc_ref[:, 2 * words : 2 * words + 2 * HEAD] += new[:rows] + new[rows:]
        return carry

    lax.fori_loop(0, blocks // 2, step, 0, unroll=4)
    for copy in kvs:
        copy.wait()
    lax.fori_loop(blocks // 2, blocks - 1, step_kv, 0, unroll=3)
    step_kv(blocks - 1, 0)
    lane = lax.broadcasted_iota(jnp.int32, (rows, 128), 1)
    a, m, l = split3(jnp.sum(ss_ref[...], axis=1, keepdims=True))
    a, m, l = a.astype(F32), m.astype(F32), l.astype(F32)
    acc_ref[:, 2 * words + 2 * HEAD :] = jnp.where(
        lane == 0, a, jnp.where(lane == 1, m, jnp.where(lane == 2, l, 0.0))
    )

    me = lax.axis_index("width")
    share = rows // nw

    def piece(s):
        return acc_ref[pl.ds(pl.multiple_of(lax.rem(me + s, nw) * share, share), share)]

    own_ref[...] = piece(0)
    for s in range(1, nw):
        sends[s - 1][...] = piece(s).astype(BF16)


def in_hbm(array):
    return pltpu.with_memory_space_constraint(array, pltpu.HBM)


def project(inputs, norm_gain, wq_packed, wq_scales, key_weight, value_weight, nw, nb):
    steps, seqs, depth = inputs.shape
    rows = steps * seqs
    words = wq_packed.shape[1] // nb
    groups = wq_scales.shape[0]
    block = 512
    blocks = depth // block
    cols = 2 * words + 3 * HEAD
    out_rows = rows // nw
    return pl.pallas_call(
        project_kernel,
        in_specs=[HBM] * 6,
        out_specs=[VMEM] * nw,
        out_shape=[jax.ShapeDtypeStruct((out_rows, cols), F32)]
        + [jax.ShapeDtypeStruct((out_rows, cols), BF16)] * (nw - 1),
        scratch_shapes=[
            pltpu.VMEM((steps, seqs, depth), BF16),
            pltpu.VMEM((1, depth), F32),
            pltpu.VMEM((blocks, block, words), jnp.int32),
            pltpu.VMEM((groups, 2 * words), F32),
            pltpu.VMEM((depth, 2 * HEAD), BF16),
            pltpu.VMEM((groups, words), F32),
            pltpu.VMEM((groups, words), F32),
            pltpu.VMEM((blocks, 2 * rows, block), BF16),
            pltpu.VMEM((rows, cols), F32),
            pltpu.VMEM((rows, 128), F32),
            pltpu.SemaphoreType.DMA((5,)),
            pltpu.SemaphoreType.DMA((blocks,)),
        ],
        compiler_params=pltpu.CompilerParams(vmem_limit_bytes=PROJECT_LIMIT),
        name="project",
    )(
        *map(
            in_hbm,
            (inputs, norm_gain.reshape(1, -1), wq_packed, wq_scales, key_weight, value_weight),
        )
    )


def weight_copies(src, dst, start, depth, sems):
    first = lax.axis_index("batch") * depth + start
    count = sems.shape[0]
    each = dst.shape[0] // count
    return [
        pltpu.make_async_copy(
            src.at[pl.ds(pl.multiple_of(first + n * each, each), each)],
            dst.at[pl.ds(n * each, each)],
            sems.at[n],
        )
        for n in range(count)
    ]


def fetch_weight(wo_weight, start, size, depth, after):
    def body(src, after, dst, sems):
        del after
        copies = weight_copies(src, dst, start, depth, sems)
        for copy in copies:
            copy.start()
        for copy in copies:
            copy.wait()

    return pl.pallas_call(
        body,
        in_specs=[HBM, ANY],
        out_specs=VMEM,
        out_shape=pltpu.VMEM((size, wo_weight.shape[1]), BF16),
        scratch_shapes=[pltpu.SemaphoreType.DMA((size // 256,))],
        compiler_params=pltpu.CompilerParams(vmem_limit_bytes=FETCH_LIMIT),
        name="fetch",
    )(in_hbm(wo_weight), after)


def attend_kernel(heads, nw, start, len_ref, own_ref, *rest):
    parts = rest[: nw - 1]
    (
        cq_ref, sq_ref, ck_ref, sk_ref, k_own, k_mate, v_own, v_mate, wo_hbm, _, out_ref, wo_ref, k_buf, v_buf, q_ref,
        m_ref, sems, wo_sems,
    ) = rest[nw - 1 :]
    each, slots, _ = k_own.shape
    b = lax.axis_index("batch")
    column = pl.ds(pl.multiple_of(b * HEAD, HEAD), HEAD)
    copies = [
        pltpu.make_async_copy(
            src.at[:, :, column], buf.at[pl.ds(place * each, each)], sems.at[n]
        )
        for n, (src, buf, place) in enumerate(
            ((k_own, k_buf, b), (k_mate, k_buf, 1 - b), (v_own, v_buf, b), (v_mate, v_buf, 1 - b))
        )
    ]
    incoming = weight_copies(wo_hbm, wo_ref, start, heads * HEAD, wo_sems)
    for copy in copies + incoming:
        copy.start()

    rows = own_ref.shape[0]
    seqs = rows // STEPS
    half = heads * HEAD // 2
    total = own_ref[...]
    for part in parts:
        total = total + part[...].astype(F32)
    squares = jnp.sum(total[:, 2 * half + 2 * HEAD :], axis=1, keepdims=True)
    total = total * lax.rsqrt(squares / D + EPS)

    lane = lax.broadcasted_iota(jnp.int32, (rows, HEAD), 1)
    left = lane < HEAD // 2
    tiles = []
    for m in range(heads // 2):
        e = total[:, m * HEAD : (m + 1) * HEAD]
        o = total[:, half + m * HEAD : half + (m + 1) * HEAD]
        tiles.append(jnp.where(left, e, pltpu.roll(o, HEAD // 2, 1)))
        tiles.append(jnp.where(left, pltpu.roll(e, HEAD // 2, 1), o))
    cos_q, sin_q, cos_k, sin_k = cq_ref[...], sq_ref[...], ck_ref[...], sk_ref[...]
    near = (lane & (HEAD // 2 - 1)) < HEAD // 4
    turned = []
    for q in tiles:
        other = jnp.where(near, pltpu.roll(q, HEAD - HEAD // 4, 1), pltpu.roll(q, HEAD // 4, 1))
        turned.append(q * cos_q + other * sin_q)
    q_all = jnp.concatenate(turned, axis=0).astype(BF16)
    row = lax.broadcasted_iota(jnp.int32, (HEAD, HEAD), 0)
    col = lax.broadcasted_iota(jnp.int32, (HEAD, HEAD), 1)
    order = jnp.where(col == 2 * (row & (HEAD // 2 - 1)) + row // (HEAD // 2), 1.0, 0.0).astype(BF16)
    q_ref[...] = jnp.dot(q_all, order, preferred_element_type=F32)
    k_new = total[:, 2 * half : 2 * half + HEAD]
    k_new = (k_new * cos_k + pltpu.roll(k_new, HEAD // 2, 1) * sin_k).astype(BF16).astype(F32)
    v_new = total[:, 2 * half + HEAD : 2 * half + 2 * HEAD].astype(BF16).astype(F32)

    for copy in copies:
        copy.wait()

    slot = lax.broadcasted_iota(jnp.int32, (STEPS * heads, slots), 1)
    later = lax.broadcasted_iota(jnp.int32, (STEPS * heads, 1), 0) >= heads
    for j in range(seqs):
        q = jnp.concatenate(
            [q_ref[pl.ds(t * seqs + j, heads, stride=rows), :] for t in range(STEPS)], axis=0
        )
        scores = lax.dot_general(
            q.astype(BF16), k_buf[j], (((1,), (1,)), ((), ())), preferred_element_type=F32
        ) * HEAD ** (-0.5)
        scores = jnp.where(slot < len_ref[j], scores, -1e30)
        first = jnp.sum(q * k_new[j : j + 1], axis=1, keepdims=True) * HEAD ** (-0.5)
        second = jnp.sum(q * k_new[seqs + j : seqs + j + 1], axis=1, keepdims=True) * HEAD ** (-0.5)
        second = jnp.where(later, second, -1e30)
        peak = jnp.maximum(jnp.max(scores, axis=1, keepdims=True), jnp.maximum(first, second))
        weights = jnp.exp(scores - peak)
        first = jnp.exp(first - peak)
        second = jnp.exp(second - peak)
        inverse = 1.0 / (jnp.sum(weights, axis=1, keepdims=True) + first + second)
        probs = (weights * inverse).astype(BF16)
        mixed = jnp.dot(probs, v_buf[j], preferred_element_type=F32)
        mixed = mixed + (first * inverse).astype(BF16).astype(F32) * v_new[j : j + 1]
        mixed = mixed + (second * inverse).astype(BF16).astype(F32) * v_new[seqs + j : seqs + j + 1]
        for t in range(STEPS):
            m_ref[pl.ds(t * seqs + j, heads, stride=rows), :] = mixed[t * heads : (t + 1) * heads]
    for n in range(heads):
        out_ref[:, n * HEAD : (n + 1) * HEAD] = m_ref[n * rows : (n + 1) * rows, :].astype(BF16)
    for copy in incoming:
        copy.wait()


def attend(own, parts, table, lengths, k_own, k_mate, v_own, v_mate, wo_weight, start, size, after, heads):
    rows = own.shape[0]
    each, slots, _ = k_own.shape
    nw = len(parts) + 1
    body = lambda *refs: attend_kernel(heads, nw, start, *refs)
    return pl.pallas_call(
        body,
        in_specs=[pl.BlockSpec(memory_space=pltpu.SMEM)] + [VMEM] * (nw + 4) + [ANY] * 4 + [HBM, ANY],
        out_specs=[VMEM, VMEM],
        out_shape=[
            jax.ShapeDtypeStruct((rows, heads * HEAD), BF16),
            pltpu.VMEM((size, wo_weight.shape[1]), BF16),
        ],
        scratch_shapes=[
            pltpu.VMEM((2 * each, slots, HEAD), BF16),
            pltpu.VMEM((2 * each, slots, HEAD), BF16),
            pltpu.VMEM((heads * rows, HEAD), F32),
            pltpu.VMEM((heads * rows, HEAD), F32),
            pltpu.SemaphoreType.DMA((4,)),
            pltpu.SemaphoreType.DMA((size // 256,)),
        ],
        compiler_params=pltpu.CompilerParams(vmem_limit_bytes=ATTEND_LIMIT),

        name="attend",
    )(lengths, own, *parts, *table, in_hbm(k_own), k_mate, in_hbm(v_own), v_mate, in_hbm(wo_weight), after)


def output_kernel(nw, count, *refs):
    pieces = refs[:nw]
    weights = refs[nw : nw + count]
    outs = refs[nw + count : 2 * nw + count]
    piece_ref, acc_ref = refs[2 * nw + count :]
    rows, depth = pieces[0].shape
    cols = weights[0].shape[1]
    place = lax.axis_index("width")
    for s in range(nw):
        piece_ref[lax.rem(place + nw - s, nw)] = pieces[s][...].astype(F32)
    lhs = piece_ref[...].reshape(nw * rows, depth).astype(BF16)
    block = 512
    for n in range(cols // block):
        span = slice(n * block, (n + 1) * block)
        acc = jnp.zeros((nw * rows, block), F32)
        first = 0
        for w_ref in weights:
            last = first + w_ref.shape[0]
            acc = acc + jnp.dot(lhs[:, first:last], w_ref[:, span], preferred_element_type=F32)
            first = last
        acc_ref[:, :, span] = acc.reshape(nw, rows, block)
    me = lax.axis_index("hidden") * lax.axis_size("batch") + lax.axis_index("batch")
    for s in range(nw):
        value = acc_ref[me ^ s].astype(outs[s].dtype)
        for t in range(STEPS):
            outs[s][t] = value[t * rows // STEPS : (t + 1) * rows // STEPS]


def output(pieces, weights):
    nw, count = len(pieces), len(weights)
    rows, depth = pieces[0].shape
    cols = weights[0].shape[1]
    body = lambda *refs: output_kernel(nw, count, *refs)
    shape = (STEPS, rows // STEPS, cols)
    return pl.pallas_call(
        body,
        in_specs=[VMEM] * (nw + count),
        out_specs=[VMEM] * nw,
        out_shape=[jax.ShapeDtypeStruct(shape, dtype) for dtype in (F32, BF16, F32, BF16)],
        scratch_shapes=[
            pltpu.VMEM((nw, rows, depth), F32),
            pltpu.VMEM((nw, rows, cols), F32),
        ],
        compiler_params=pltpu.CompilerParams(vmem_limit_bytes=OUTPUT_LIMIT),
        name="output",
    )(*pieces, *weights)


def rotary_tables(positions):
    lane = jnp.arange(HEAD, dtype=jnp.int32)
    parity = 2 * (lane % (HEAD // 2)) + lane // (HEAD // 2)
    out = []
    for dim in (parity, lane):
        pair = (dim % (HEAD // 2)).astype(F32)
        freq = 500000.0 ** (-2.0 * pair / HEAD)
        angle = positions.astype(F32)[:, None] * freq[None, :]
        sign = jnp.where(dim < HEAD // 2, -1.0, 1.0)[None, :]
        out += [jnp.cos(angle), jnp.sin(angle) * sign]
    return out


def split_heads(
    inputs,
    norm_gain,
    wq_packed,
    wq_scales,
    key_weight,
    value_weight,
    wo_weight,
    key_cache,
    value_cache,
    lengths,
):
    nw, nh, nb = lax.axis_size("width"), lax.axis_size("hidden"), lax.axis_size("batch")
    swap = [(0, 1), (1, 0)]
    k_mate = lax.ppermute(key_cache, "batch", swap)
    v_mate = lax.ppermute(value_cache, "batch", swap)
    len_mate = lax.ppermute(lengths, "batch", swap)
    first = lax.axis_index("batch") == 0
    len_all = jnp.where(
        first, jnp.concatenate([lengths, len_mate]), jnp.concatenate([len_mate, lengths])
    )
    positions = jnp.concatenate([len_all + step for step in range(STEPS)])
    table = rotary_tables(positions)

    own, *sends = project(
        inputs, norm_gain, wq_packed, wq_scales, key_weight, value_weight, nw, nb
    )
    own, k_mate, v_mate, *sends = lax.optimization_barrier((own, k_mate, v_mate, *sends))
    parts = [
        lax.ppermute(piece, "width", [(i, (i + s) % nw) for i in range(nw)])
        for s, piece in enumerate(sends, 1)
    ]
    heads = 2 * wq_packed.shape[1] // nb // HEAD
    depth = heads * HEAD
    early, middle, late = EARLY * depth // 8, MIDDLE * depth // 8, LATE * depth // 8
    w_early = fetch_weight(wo_weight, 0, early, depth, own)
    mixed, w_middle = attend(
        own, parts, table, len_all, key_cache, k_mate, value_cache, v_mate, wo_weight, early, middle,
        w_early, heads,
    )
    w_late = fetch_weight(wo_weight, early + middle, late, depth, mixed)
    pieces = [mixed] + [
        lax.ppermute(mixed, "width", [(i, (i + s) % nw) for i in range(nw)]) for s in range(1, nw)
    ]
    here, across_core, across_chip, across_both = output(pieces, [w_early, w_middle, w_late])
    relay = lax.ppermute(across_both, "batch", swap)
    near = lax.ppermute(across_core, "batch", swap)
    leaving = (across_chip + relay.astype(F32)).astype(BF16)
    far = lax.ppermute(leaving, "hidden", swap)
    sums = here + near.astype(F32) + far.astype(F32)
    return sums.astype(BF16)


def solution(mesh):
    sizes = mesh.shape

    def on_device(*args):
        kv_local = args[4].shape[1] // HEAD
        fits = (
            sizes["batch"] == 2
            and sizes["hidden"] == 2
            and kv_local == 2
            and sizes["width"] == sizes["hidden"] * sizes["batch"]
            and args[0].shape[1] // sizes["width"] == 2 * args[9].shape[0]
            and args[0].shape[2] % 512 == 0
            and STEPS * args[0].shape[1] // sizes["width"] % 8 == 0
        )
        return split_heads(*args) if fits else general(*args)

    in_specs = (
        P(None, "groups", "width"),
        P("width"),
        P("width", "hidden"),
        P("width", "hidden"),
        P("width", "hidden"),
        P("width", "hidden"),
        P("hidden", "width"),
        P(("groups", "width", "batch"), None, "hidden"),
        P(("groups", "width", "batch"), None, "hidden"),
        P(("groups", "width", "batch")),
    )
    out_specs = P(None, ("groups", "hidden", "batch"), "width")
    return jax.shard_map(
        on_device, mesh=mesh, in_specs=in_specs, out_specs=out_specs, check_vma=False
    )
```

```python
import jax
import jax.numpy as jnp
from jax import lax
from jax.experimental import pallas as pl
from jax.experimental.pallas import tpu as pltpu
from jax.sharding import PartitionSpec as P

D = 16384
HEAD = 128
STEPS = 2
EPS = 1e-05
BF16 = jnp.bfloat16
F32 = jnp.float32
MIB = 1024 * 1024
PROJECT_LIMIT = 26 * MIB
ATTEND_LIMIT = 10 * MIB
OUTPUT_LIMIT = 10 * MIB
FETCH_LIMIT = 1 * MIB
EARLY, MIDDLE, LATE = 2, 3, 3
HBM = pl.BlockSpec(memory_space=pltpu.HBM)
ANY = pl.BlockSpec(memory_space=pl.ANY)
VMEM = pl.BlockSpec(memory_space=pltpu.VMEM)


def unpack_weights(packed, scales, bits, per_word):
    shifts = jnp.arange(per_word, dtype=jnp.int32) * bits
    codes = packed[:, :, None] >> shifts & (1 << bits) - 1
    values = (codes - (1 << bits - 1)).astype(jnp.float32)
    values = values.reshape(packed.shape[0], packed.shape[1] * per_word)
    group_rows = packed.shape[0] // scales.shape[0]
    values = values.reshape(scales.shape[0], group_rows, values.shape[1]) * scales[:, None, :]
    return values.reshape(packed.shape[0], -1)


def rotate_heads(field, positions):
    half = field.shape[-1] // 2
    freq = 500000.0 ** (-2.0 * jnp.arange(half, dtype=jnp.float32) / field.shape[-1])
    angle = positions.astype(jnp.float32)[:, None] * freq[None, :]
    cosine = jnp.cos(angle)[:, None, :]
    sine = jnp.sin(angle)[:, None, :]
    first = field[..., :half]
    second = field[..., half:]
    return jnp.concatenate(
        [first * cosine - second * sine, second * cosine + first * sine], axis=-1
    )


def general(
    inputs,
    norm_gain,
    wq_packed,
    wq_scales,
    key_weight,
    value_weight,
    wo_weight,
    key_cache,
    value_cache,
    lengths,
):
    high = lax.Precision.HIGHEST
    w_query = unpack_weights(wq_packed, wq_scales, 4, 2)
    w_output = wo_weight.astype(jnp.float32)
    w_joined = jnp.concatenate(
        [w_query, key_weight.astype(jnp.float32), value_weight.astype(jnp.float32)], axis=1
    )
    seq_local = lengths.shape[0]
    slots = key_cache.shape[1]
    kv_local = key_weight.shape[1] // HEAD
    q_local = w_query.shape[1] // HEAD
    repeat = q_local // kv_local
    cols_local = inputs.shape[2]
    keys_all = key_cache
    values_all = value_cache
    slot_ids = jnp.arange(slots, dtype=jnp.int32)
    results = []
    for step in range(STEPS):
        rows = inputs[step].astype(jnp.float32)
        width_count = lax.axis_size("width")
        batch_count = lax.axis_size("batch")
        arranged = rows.reshape(width_count, batch_count, seq_local, cols_local)
        rows = lax.dynamic_index_in_dim(arranged, lax.axis_index("batch"), 1, keepdims=False)
        rows = rows.reshape(width_count * seq_local, cols_local)
        squares = jnp.sum(rows * rows, axis=1)
        total = lax.psum(squares, "width")
        scale = lax.rsqrt(total / D + EPS)
        normed = rows * scale[:, None] * norm_gain[None, :]
        partial_value = jnp.dot(
            normed, w_joined, precision=high, preferred_element_type=jnp.float32
        )
        projected = lax.psum_scatter(partial_value, "width", scatter_dimension=0, tiled=True)
        positions = lengths + step
        q_cols = q_local * HEAD
        kv_cols = kv_local * HEAD
        queries = rotate_heads(
            projected[:, :q_cols].reshape(seq_local, q_local, HEAD), positions
        ).astype(jnp.bfloat16)
        keys_new = rotate_heads(
            projected[:, q_cols : q_cols + kv_cols].reshape(seq_local, kv_local, HEAD), positions
        )
        keys_new = keys_new.reshape(seq_local, kv_cols).astype(jnp.bfloat16)
        values_new = projected[:, q_cols + kv_cols :].astype(jnp.bfloat16)
        written = slot_ids[None, :, None] == positions[:, None, None]
        keys_all = jnp.where(written, keys_new[:, None, :], keys_all)
        values_all = jnp.where(written, values_new[:, None, :], values_all)
        query_heads = queries.reshape(seq_local, kv_local, repeat, HEAD)
        key_heads = keys_all.reshape(seq_local, slots, kv_local, HEAD)
        value_heads = values_all.reshape(seq_local, slots, kv_local, HEAD)
        scores = jnp.einsum(
            "bgrd,bsgd->bgrs", query_heads, key_heads, preferred_element_type=jnp.float32
        ) * HEAD ** (-0.5)
        valid = slot_ids[None, None, None, :] <= positions[:, None, None, None]
        scores = jnp.where(valid, scores, -1e30)
        peak = jnp.max(scores, axis=-1, keepdims=True)
        weights = jnp.exp(scores - peak)
        total_weight = jnp.sum(weights, axis=-1, keepdims=True)
        probs = (weights / total_weight).astype(jnp.bfloat16)
        mixed = jnp.einsum(
            "bgrs,bsgd->bgrd", probs, value_heads, preferred_element_type=jnp.float32
        )
        mixed = mixed.reshape(seq_local, q_cols).astype(jnp.bfloat16)
        out_terms = jnp.dot(
            lax.all_gather(mixed, ("width", "batch"), axis=0, tiled=True).astype(jnp.float32),
            w_output,
            precision=high,
            preferred_element_type=jnp.float32,
        )
        head_sums = lax.psum_scatter(out_terms, "hidden", scatter_dimension=0, tiled=True)
        share = head_sums.shape[0] // lax.axis_size("batch")
        attended = lax.dynamic_slice_in_dim(head_sums, lax.axis_index("batch") * share, share, 0)
        results.append(attended.astype(jnp.bfloat16))
    return jnp.stack(results)


def split3(value):
    hi = value.astype(BF16)
    rest = value - hi.astype(F32)
    mid = rest.astype(BF16)
    low = (rest - mid.astype(F32)).astype(BF16)
    return hi, mid, low


def project_kernel(
    x_hbm, gain_hbm, wq_hbm, scale_hbm, kw_hbm, vw_hbm, own_ref, *rest
):
    nw = len(rest) - 11
    sends = rest[: nw - 1]
    (
        x_ref, gain_ref, wq_ref, scale_ref, kv_ref, se_ref, so_ref, y_ref, acc_ref, ss_ref, sems,
        block_sems,
    ) = rest[nw - 1 :]
    steps, seqs, depth = x_ref.shape
    rows = steps * seqs
    each = seqs // nw
    blocks, block, words = wq_ref.shape
    groups = se_ref.shape[0]
    per_block = groups // blocks
    group = block // per_block
    b = lax.axis_index("batch")

    def columns(n):
        return pl.ds(pl.multiple_of(b * n, n), n)

    def fetch(i):
        return pltpu.make_async_copy(
            wq_hbm.at[pl.ds(pl.multiple_of(i * block, block), block), columns(words)],
            wq_ref.at[i],
            block_sems.at[i],
        )

    scale_copy = pltpu.make_async_copy(scale_hbm.at[:, columns(2 * words)], scale_ref, sems.at[0])
    others = [
        pltpu.make_async_copy(gain_hbm, gain_ref, sems.at[1]),
        pltpu.make_async_copy(x_hbm, x_ref, sems.at[4]),
    ]
    kvs = [
        pltpu.make_async_copy(kw_hbm.at[:, columns(HEAD)], kv_ref.at[:, :HEAD], sems.at[2]),
        pltpu.make_async_copy(vw_hbm.at[:, columns(HEAD)], kv_ref.at[:, HEAD:], sems.at[3]),
    ]
    scale_copy.start()
    for copy in others:
        copy.start()
    for i in range(3):
        fetch(i).start()

    acc_ref[...] = jnp.zeros_like(acc_ref)
    ss_ref[...] = jnp.zeros_like(ss_ref)
    row = lax.broadcasted_iota(jnp.int32, (256, 256), 0)
    col = lax.broadcasted_iota(jnp.int32, (256, 256), 1)
    pick = jnp.where(row == 2 * (col & 127) + (col >> 7), 1.0, 0.0).astype(BF16)
    scale_copy.wait()
    for c in range(words // 128):
        terms = split3(scale_ref[:, c * 256 : (c + 1) * 256])
        parts = [jnp.dot(term, pick, preferred_element_type=F32) for term in terms]
        both = parts[0] + (parts[1] + parts[2])
        se_ref[:, c * 128 : (c + 1) * 128] = both[:, :128]
        so_ref[:, c * 128 : (c + 1) * 128] = both[:, 128:]
    for copy in others:
        copy.wait()

    chunk = 512

    def step(i, carry):
        here = pl.ds(pl.multiple_of(i * block, block), block)
        x = x_ref[:, :, here].astype(F32)
        x = jnp.concatenate(
            [x[t, v * each : (v + 1) * each] for v in range(nw) for t in range(steps)], axis=0
        )
        y = x * gain_ref[:, here]
        hi = y.astype(BF16)
        low = (y - hi.astype(F32)).astype(BF16)
        lhs = jnp.concatenate([hi, low], axis=0)
        y_ref[i] = lhs
        squares = x * x
        ss_ref[...] += sum(squares[:, c * 128 : (c + 1) * 128] for c in range(block // 128))
        sums = [
            8.0 * jnp.sum(y[:, g * group : (g + 1) * group], axis=1, keepdims=True)
            for g in range(per_block)
        ]
        fetch(i).wait()

        @pl.when(i + 3 < blocks)
        def _():
            fetch(i + 3).start()

        @pl.when(i == 0)
        def _():
            for copy in kvs:
                copy.start()

        for c in range(words // chunk):
            cols = slice(c * chunk, (c + 1) * chunk)
            even = jnp.zeros((rows, chunk), F32)
            odd = jnp.zeros((rows, chunk), F32)
            for g in range(per_block):
                span = slice(g * group, (g + 1) * group)
                word = wq_ref[i, span, cols]
                both = word.astype(F32).astype(BF16)
                upper = (word >> 4).astype(F32).astype(BF16)
                left = lhs[:, span]
                p = jnp.dot(left, both, preferred_element_type=F32)
                u = jnp.dot(left, upper, preferred_element_type=F32)
                p = p[:rows] + p[rows:]
                u = u[:rows] + u[rows:]
                at = pl.ds(i * per_block + g, 1)
                even = even + (p - 16.0 * u - sums[g]) * se_ref[at, cols]
                odd = odd + (u - sums[g]) * so_ref[at, cols]
            acc_ref[:, cols] += even
            acc_ref[:, words + c * chunk : words + (c + 1) * chunk] += odd
        return carry

    def step_kv(i, carry):
        step(i, carry)
        new = jnp.zeros((2 * rows, 2 * HEAD), F32)
        for n in range(2):
            j = 2 * i - blocks + n
            at = pl.ds(pl.multiple_of(j * block, block), block)
            new = new + jnp.dot(y_ref[j], kv_ref[at], preferred_element_type=F32)
        acc_ref[:, 2 * words : 2 * words + 2 * HEAD] += new[:rows] + new[rows:]
        return carry

    lax.fori_loop(0, blocks // 2, step, 0, unroll=4)
    for copy in kvs:
        copy.wait()
    lax.fori_loop(blocks // 2, blocks - 1, step_kv, 0, unroll=3)
    step_kv(blocks - 1, 0)
    lane = lax.broadcasted_iota(jnp.int32, (rows, 128), 1)
    a, m, l = split3(jnp.sum(ss_ref[...], axis=1, keepdims=True))
    a, m, l = a.astype(F32), m.astype(F32), l.astype(F32)
    acc_ref[:, 2 * words + 2 * HEAD :] = jnp.where(
        lane == 0, a, jnp.where(lane == 1, m, jnp.where(lane == 2, l, 0.0))
    )

    me = lax.axis_index("width")
    share = rows // nw

    def piece(s):
        return acc_ref[pl.ds(pl.multiple_of((me ^ s) * share, share), share)]

    own_ref[...] = piece(0)
    for s in range(1, nw):
        sends[s - 1][...] = piece(s).astype(BF16)


def in_hbm(array):
    return pltpu.with_memory_space_constraint(array, pltpu.HBM)


def project(inputs, norm_gain, wq_packed, wq_scales, key_weight, value_weight, nw, nb):
    steps, seqs, depth = inputs.shape
    rows = steps * seqs
    words = wq_packed.shape[1] // nb
    groups = wq_scales.shape[0]
    block = 512
    blocks = depth // block
    cols = 2 * words + 3 * HEAD
    out_rows = rows // nw
    return pl.pallas_call(
        project_kernel,
        in_specs=[HBM] * 6,
        out_specs=[VMEM] * nw,
        out_shape=[jax.ShapeDtypeStruct((out_rows, cols), F32)]
        + [jax.ShapeDtypeStruct((out_rows, cols), BF16)] * (nw - 1),
        scratch_shapes=[
            pltpu.VMEM((steps, seqs, depth), BF16),
            pltpu.VMEM((1, depth), F32),
            pltpu.VMEM((blocks, block, words), jnp.int32),
            pltpu.VMEM((groups, 2 * words), F32),
            pltpu.VMEM((depth, 2 * HEAD), BF16),
            pltpu.VMEM((groups, words), F32),
            pltpu.VMEM((groups, words), F32),
            pltpu.VMEM((blocks, 2 * rows, block), BF16),
            pltpu.VMEM((rows, cols), F32),
            pltpu.VMEM((rows, 128), F32),
            pltpu.SemaphoreType.DMA((5,)),
            pltpu.SemaphoreType.DMA((blocks,)),
        ],
        compiler_params=pltpu.CompilerParams(vmem_limit_bytes=PROJECT_LIMIT),
        name="project",
    )(
        *map(
            in_hbm,
            (inputs, norm_gain.reshape(1, -1), wq_packed, wq_scales, key_weight, value_weight),
        )
    )


def weight_copies(src, dst, start, depth, sems):
    first = lax.axis_index("batch") * depth + start
    count = sems.shape[0]
    each = dst.shape[0] // count
    return [
        pltpu.make_async_copy(
            src.at[pl.ds(pl.multiple_of(first + n * each, each), each)],
            dst.at[pl.ds(n * each, each)],
            sems.at[n],
        )
        for n in range(count)
    ]


def fetch_weight(wo_weight, start, size, depth, after):
    def body(src, after, dst, sems):
        del after
        copies = weight_copies(src, dst, start, depth, sems)
        for copy in copies:
            copy.start()
        for copy in copies:
            copy.wait()

    return pl.pallas_call(
        body,
        in_specs=[HBM, ANY],
        out_specs=VMEM,
        out_shape=pltpu.VMEM((size, wo_weight.shape[1]), BF16),
        scratch_shapes=[pltpu.SemaphoreType.DMA((size // 256,))],
        compiler_params=pltpu.CompilerParams(vmem_limit_bytes=FETCH_LIMIT),
        name="fetch",
    )(in_hbm(wo_weight), after)


def attend_kernel(heads, nw, start, len_ref, own_ref, *rest):
    parts = rest[: nw - 1]
    (
        cq_ref, sq_ref, ck_ref, sk_ref, k_own, k_mate, v_own, v_mate, wo_hbm, _, out_ref, wo_ref, k_buf, v_buf, q_ref,
        m_ref, sems, wo_sems,
    ) = rest[nw - 1 :]
    held, slots, _ = k_own.shape
    b = lax.axis_index("batch")
    column = pl.ds(pl.multiple_of(b * HEAD, HEAD), HEAD)
    copies = [
        pltpu.make_async_copy(
            src.at[:, :, column], buf.at[pl.ds(place * held, held)], sems.at[n]
        )
        for n, (src, buf, place) in enumerate(
            ((k_own, k_buf, b), (k_mate, k_buf, 1 - b), (v_own, v_buf, b), (v_mate, v_buf, 1 - b))
        )
    ]
    incoming = weight_copies(wo_hbm, wo_ref, start, heads * HEAD, wo_sems)
    for copy in copies + incoming:
        copy.start()

    rows = own_ref.shape[0]
    seqs = rows // STEPS
    half = heads * HEAD // 2
    total = own_ref[...]
    for part in parts:
        total = total + part[...].astype(F32)
    squares = jnp.sum(total[:, 2 * half + 2 * HEAD :], axis=1, keepdims=True)
    total = total * lax.rsqrt(squares / D + EPS)

    lane = lax.broadcasted_iota(jnp.int32, (rows, HEAD), 1)
    left = lane < HEAD // 2
    tiles = []
    for m in range(heads // 2):
        e = total[:, m * HEAD : (m + 1) * HEAD]
        o = total[:, half + m * HEAD : half + (m + 1) * HEAD]
        tiles.append(jnp.where(left, e, pltpu.roll(o, HEAD // 2, 1)))
        tiles.append(jnp.where(left, pltpu.roll(e, HEAD // 2, 1), o))
    cos_q, sin_q, cos_k, sin_k = cq_ref[...], sq_ref[...], ck_ref[...], sk_ref[...]
    near = (lane & (HEAD // 2 - 1)) < HEAD // 4
    turned = []
    for q in tiles:
        other = jnp.where(near, pltpu.roll(q, HEAD - HEAD // 4, 1), pltpu.roll(q, HEAD // 4, 1))
        turned.append(q * cos_q + other * sin_q)
    q_all = jnp.concatenate(turned, axis=0).astype(BF16)
    row = lax.broadcasted_iota(jnp.int32, (HEAD, HEAD), 0)
    col = lax.broadcasted_iota(jnp.int32, (HEAD, HEAD), 1)
    order = jnp.where(col == 2 * (row & (HEAD // 2 - 1)) + row // (HEAD // 2), 1.0, 0.0).astype(BF16)
    q_ref[...] = jnp.dot(q_all, order, preferred_element_type=F32)
    k_new = total[:, 2 * half : 2 * half + HEAD]
    k_new = (k_new * cos_k + pltpu.roll(k_new, HEAD // 2, 1) * sin_k).astype(BF16).astype(F32)
    v_new = total[:, 2 * half + HEAD : 2 * half + 2 * HEAD].astype(BF16).astype(F32)

    for copy in copies:
        copy.wait()

    each = STEPS * heads
    queries = [
        jnp.concatenate(
            [q_ref[pl.ds(t * seqs + j, heads, stride=rows), :] for t in range(STEPS)], axis=0
        )
        for j in range(seqs)
    ]
    scores = jnp.concatenate(
        [
            lax.dot_general(
                queries[j].astype(BF16), k_buf[j], (((1,), (1,)), ((), ())),
                preferred_element_type=F32,
            )
            for j in range(seqs)
        ],
        axis=0,
    ) * HEAD ** (-0.5)
    row = lax.broadcasted_iota(jnp.int32, (seqs * each, 1), 0)
    filled = jnp.full((seqs * each, 1), len_ref[seqs - 1], jnp.int32)
    for j in range(seqs - 1, 0, -1):
        filled = jnp.where(row < j * each, len_ref[j - 1], filled)
    slot = lax.broadcasted_iota(jnp.int32, (seqs * each, slots), 1)
    scores = jnp.where(slot < filled, scores, -1e30)

    def fresh(t):
        dots = [
            jnp.sum(queries[j] * k_new[t * seqs + j : t * seqs + j + 1], axis=1, keepdims=True)
            for j in range(seqs)
        ]
        return jnp.concatenate(dots, axis=0) * HEAD ** (-0.5)

    first = fresh(0)
    second = jnp.where(lax.rem(row, each) >= heads, fresh(1), -1e30)
    peak = jnp.maximum(jnp.max(scores, axis=1, keepdims=True), jnp.maximum(first, second))
    weights = jnp.exp(scores - peak)
    first = jnp.exp(first - peak)
    second = jnp.exp(second - peak)
    inverse = 1.0 / (jnp.sum(weights, axis=1, keepdims=True) + first + second)
    probs = (weights * inverse).astype(BF16)
    first = (first * inverse).astype(BF16).astype(F32)
    second = (second * inverse).astype(BF16).astype(F32)
    for j in range(seqs):
        span = slice(j * each, (j + 1) * each)
        mixed = jnp.dot(probs[span], v_buf[j], preferred_element_type=F32)
        mixed = mixed + first[span] * v_new[j : j + 1]
        mixed = mixed + second[span] * v_new[seqs + j : seqs + j + 1]
        for t in range(STEPS):
            m_ref[pl.ds(t * seqs + j, heads, stride=rows), :] = mixed[t * heads : (t + 1) * heads]
    for n in range(heads):
        out_ref[:, n * HEAD : (n + 1) * HEAD] = m_ref[n * rows : (n + 1) * rows, :].astype(BF16)
    for copy in incoming:
        copy.wait()


def attend(own, parts, table, lengths, k_own, k_mate, v_own, v_mate, wo_weight, start, size, after, heads):
    rows = own.shape[0]
    each, slots, _ = k_own.shape
    nw = len(parts) + 1
    body = lambda *refs: attend_kernel(heads, nw, start, *refs)
    return pl.pallas_call(
        body,
        in_specs=[pl.BlockSpec(memory_space=pltpu.SMEM)] + [VMEM] * (nw + 4) + [ANY] * 4 + [HBM, ANY],
        out_specs=[VMEM, VMEM],
        out_shape=[
            jax.ShapeDtypeStruct((rows, heads * HEAD), BF16),
            pltpu.VMEM((size, wo_weight.shape[1]), BF16),
        ],
        scratch_shapes=[
            pltpu.VMEM((2 * each, slots, HEAD), BF16),
            pltpu.VMEM((2 * each, slots, HEAD), BF16),
            pltpu.VMEM((heads * rows, HEAD), F32),
            pltpu.VMEM((heads * rows, HEAD), F32),
            pltpu.SemaphoreType.DMA((4,)),
            pltpu.SemaphoreType.DMA((size // 256,)),
        ],
        compiler_params=pltpu.CompilerParams(vmem_limit_bytes=ATTEND_LIMIT),

        name="attend",
    )(lengths, own, *parts, *table, in_hbm(k_own), k_mate, in_hbm(v_own), v_mate, in_hbm(wo_weight), after)


def output_kernel(nw, count, *refs):
    pieces = refs[:nw]
    weights = refs[nw : nw + count]
    outs = refs[nw + count : 2 * nw + count]
    piece_ref, acc_ref = refs[2 * nw + count :]
    rows, depth = pieces[0].shape
    cols = weights[0].shape[1]
    place = lax.axis_index("width")
    for s in range(nw):
        piece_ref[place ^ s] = pieces[s][...].astype(F32)
    lhs = piece_ref[...].reshape(nw * rows, depth).astype(BF16)
    block = 512
    for n in range(cols // block):
        span = slice(n * block, (n + 1) * block)
        acc = jnp.zeros((nw * rows, block), F32)
        first = 0
        for w_ref in weights:
            last = first + w_ref.shape[0]
            acc = acc + jnp.dot(lhs[:, first:last], w_ref[:, span], preferred_element_type=F32)
            first = last
        acc_ref[:, :, span] = acc.reshape(nw, rows, block)
    me = lax.axis_index("hidden") * lax.axis_size("batch") + lax.axis_index("batch")
    for s in range(nw):
        value = acc_ref[me ^ s].astype(outs[s].dtype)
        for t in range(STEPS):
            outs[s][t] = value[t * rows // STEPS : (t + 1) * rows // STEPS]


def output(pieces, weights):
    nw, count = len(pieces), len(weights)
    rows, depth = pieces[0].shape
    cols = weights[0].shape[1]
    body = lambda *refs: output_kernel(nw, count, *refs)
    shape = (STEPS, rows // STEPS, cols)
    return pl.pallas_call(
        body,
        in_specs=[VMEM] * (nw + count),
        out_specs=[VMEM] * nw,
        out_shape=[jax.ShapeDtypeStruct(shape, dtype) for dtype in (F32, BF16, F32, BF16)],
        scratch_shapes=[
            pltpu.VMEM((nw, rows, depth), F32),
            pltpu.VMEM((nw, rows, cols), F32),
        ],
        compiler_params=pltpu.CompilerParams(vmem_limit_bytes=OUTPUT_LIMIT),
        name="output",
    )(*pieces, *weights)


def rotary_tables(positions):
    lane = jnp.arange(HEAD, dtype=jnp.int32)
    parity = 2 * (lane % (HEAD // 2)) + lane // (HEAD // 2)
    out = []
    for dim in (parity, lane):
        pair = (dim % (HEAD // 2)).astype(F32)
        freq = 500000.0 ** (-2.0 * pair / HEAD)
        angle = positions.astype(F32)[:, None] * freq[None, :]
        sign = jnp.where(dim < HEAD // 2, -1.0, 1.0)[None, :]
        out += [jnp.cos(angle), jnp.sin(angle) * sign]
    return out


def split_heads(
    inputs,
    norm_gain,
    wq_packed,
    wq_scales,
    key_weight,
    value_weight,
    wo_weight,
    key_cache,
    value_cache,
    lengths,
):
    nw, nh, nb = lax.axis_size("width"), lax.axis_size("hidden"), lax.axis_size("batch")
    swap = [(0, 1), (1, 0)]
    k_mate = lax.ppermute(key_cache, "batch", swap)
    v_mate = lax.ppermute(value_cache, "batch", swap)
    len_mate = lax.ppermute(lengths, "batch", swap)
    first = lax.axis_index("batch") == 0
    len_all = jnp.where(
        first, jnp.concatenate([lengths, len_mate]), jnp.concatenate([len_mate, lengths])
    )
    positions = jnp.concatenate([len_all + step for step in range(STEPS)])
    table = rotary_tables(positions)

    own, *sends = project(
        inputs, norm_gain, wq_packed, wq_scales, key_weight, value_weight, nw, nb
    )
    own, k_mate, v_mate, *sends = lax.optimization_barrier((own, k_mate, v_mate, *sends))
    parts = [
        lax.ppermute(piece, "width", [(i, i ^ s) for i in range(nw)])
        for s, piece in enumerate(sends, 1)
    ]
    heads = 2 * wq_packed.shape[1] // nb // HEAD
    depth = heads * HEAD
    early, middle, late = EARLY * depth // 8, MIDDLE * depth // 8, LATE * depth // 8
    w_early = fetch_weight(wo_weight, 0, early, depth, own)
    mixed, w_middle = attend(
        own, parts[::-1], table, len_all, key_cache, k_mate, value_cache, v_mate, wo_weight, early, middle,
        w_early, heads,
    )
    w_late = fetch_weight(wo_weight, early + middle, late, depth, mixed)
    pieces = [mixed] + [
        lax.ppermute(mixed, "width", [(i, i ^ s) for i in range(nw)]) for s in range(1, nw)
    ]
    here, across_core, across_chip, across_both = output(pieces, [w_early, w_middle, w_late])
    relay = lax.ppermute(across_both, "batch", swap)
    near = lax.ppermute(across_core, "batch", swap)
    leaving = (across_chip + relay.astype(F32)).astype(BF16)
    far = lax.ppermute(leaving, "hidden", swap)
    sums = here + near.astype(F32) + far.astype(F32)
    return sums.astype(BF16)


def solution(mesh):
    sizes = mesh.shape

    def on_device(*args):
        kv_local = args[4].shape[1] // HEAD
        fits = (
            sizes["batch"] == 2
            and sizes["hidden"] == 2
            and kv_local == 2
            and sizes["width"] == sizes["hidden"] * sizes["batch"]
            and args[0].shape[1] // sizes["width"] == 2 * args[9].shape[0]
            and args[0].shape[2] % 512 == 0
            and STEPS * args[0].shape[1] // sizes["width"] % 8 == 0
        )
        return split_heads(*args) if fits else general(*args)

    in_specs = (
        P(None, "groups", "width"),
        P("width"),
        P("width", "hidden"),
        P("width", "hidden"),
        P("width", "hidden"),
        P("width", "hidden"),
        P("hidden", "width"),
        P(("groups", "width", "batch"), None, "hidden"),
        P(("groups", "width", "batch"), None, "hidden"),
        P(("groups", "width", "batch")),
    )
    out_specs = P(None, ("groups", "hidden", "batch"), "width")
    return jax.shard_map(
        on_device, mesh=mesh, in_specs=in_specs, out_specs=out_specs, check_vma=False
    )
```

```python
import jax
import jax.numpy as jnp
from jax import lax
from jax.experimental import pallas as pl
from jax.experimental.pallas import tpu as pltpu
from jax.sharding import PartitionSpec as P

D = 16384
HEAD = 128
STEPS = 2
EPS = 1e-05
BF16 = jnp.bfloat16
F32 = jnp.float32
MIB = 1024 * 1024
PROJECT_LIMIT = 26 * MIB
ATTEND_LIMIT = 10 * MIB
OUTPUT_LIMIT = 10 * MIB
FETCH_LIMIT = 1 * MIB
EARLY, MIDDLE, LATE = 2, 3, 3
HBM = pl.BlockSpec(memory_space=pltpu.HBM)
ANY = pl.BlockSpec(memory_space=pl.ANY)
VMEM = pl.BlockSpec(memory_space=pltpu.VMEM)


def unpack_weights(packed, scales, bits, per_word):
    shifts = jnp.arange(per_word, dtype=jnp.int32) * bits
    codes = packed[:, :, None] >> shifts & (1 << bits) - 1
    values = (codes - (1 << bits - 1)).astype(jnp.float32)
    values = values.reshape(packed.shape[0], packed.shape[1] * per_word)
    group_rows = packed.shape[0] // scales.shape[0]
    values = values.reshape(scales.shape[0], group_rows, values.shape[1]) * scales[:, None, :]
    return values.reshape(packed.shape[0], -1)


def rotate_heads(field, positions):
    half = field.shape[-1] // 2
    freq = 500000.0 ** (-2.0 * jnp.arange(half, dtype=jnp.float32) / field.shape[-1])
    angle = positions.astype(jnp.float32)[:, None] * freq[None, :]
    cosine = jnp.cos(angle)[:, None, :]
    sine = jnp.sin(angle)[:, None, :]
    first = field[..., :half]
    second = field[..., half:]
    return jnp.concatenate(
        [first * cosine - second * sine, second * cosine + first * sine], axis=-1
    )


def general(
    inputs,
    norm_gain,
    wq_packed,
    wq_scales,
    key_weight,
    value_weight,
    wo_weight,
    key_cache,
    value_cache,
    lengths,
):
    high = lax.Precision.HIGHEST
    w_query = unpack_weights(wq_packed, wq_scales, 4, 2)
    w_output = wo_weight.astype(jnp.float32)
    w_joined = jnp.concatenate(
        [w_query, key_weight.astype(jnp.float32), value_weight.astype(jnp.float32)], axis=1
    )
    seq_local = lengths.shape[0]
    slots = key_cache.shape[1]
    kv_local = key_weight.shape[1] // HEAD
    q_local = w_query.shape[1] // HEAD
    repeat = q_local // kv_local
    cols_local = inputs.shape[2]
    keys_all = key_cache
    values_all = value_cache
    slot_ids = jnp.arange(slots, dtype=jnp.int32)
    results = []
    for step in range(STEPS):
        rows = inputs[step].astype(jnp.float32)
        width_count = lax.axis_size("width")
        batch_count = lax.axis_size("batch")
        arranged = rows.reshape(width_count, batch_count, seq_local, cols_local)
        rows = lax.dynamic_index_in_dim(arranged, lax.axis_index("batch"), 1, keepdims=False)
        rows = rows.reshape(width_count * seq_local, cols_local)
        squares = jnp.sum(rows * rows, axis=1)
        total = lax.psum(squares, "width")
        scale = lax.rsqrt(total / D + EPS)
        normed = rows * scale[:, None] * norm_gain[None, :]
        partial_value = jnp.dot(
            normed, w_joined, precision=high, preferred_element_type=jnp.float32
        )
        projected = lax.psum_scatter(partial_value, "width", scatter_dimension=0, tiled=True)
        positions = lengths + step
        q_cols = q_local * HEAD
        kv_cols = kv_local * HEAD
        queries = rotate_heads(
            projected[:, :q_cols].reshape(seq_local, q_local, HEAD), positions
        ).astype(jnp.bfloat16)
        keys_new = rotate_heads(
            projected[:, q_cols : q_cols + kv_cols].reshape(seq_local, kv_local, HEAD), positions
        )
        keys_new = keys_new.reshape(seq_local, kv_cols).astype(jnp.bfloat16)
        values_new = projected[:, q_cols + kv_cols :].astype(jnp.bfloat16)
        written = slot_ids[None, :, None] == positions[:, None, None]
        keys_all = jnp.where(written, keys_new[:, None, :], keys_all)
        values_all = jnp.where(written, values_new[:, None, :], values_all)
        query_heads = queries.reshape(seq_local, kv_local, repeat, HEAD)
        key_heads = keys_all.reshape(seq_local, slots, kv_local, HEAD)
        value_heads = values_all.reshape(seq_local, slots, kv_local, HEAD)
        scores = jnp.einsum(
            "bgrd,bsgd->bgrs", query_heads, key_heads, preferred_element_type=jnp.float32
        ) * HEAD ** (-0.5)
        valid = slot_ids[None, None, None, :] <= positions[:, None, None, None]
        scores = jnp.where(valid, scores, -1e30)
        peak = jnp.max(scores, axis=-1, keepdims=True)
        weights = jnp.exp(scores - peak)
        total_weight = jnp.sum(weights, axis=-1, keepdims=True)
        probs = (weights / total_weight).astype(jnp.bfloat16)
        mixed = jnp.einsum(
            "bgrs,bsgd->bgrd", probs, value_heads, preferred_element_type=jnp.float32
        )
        mixed = mixed.reshape(seq_local, q_cols).astype(jnp.bfloat16)
        out_terms = jnp.dot(
            lax.all_gather(mixed, ("width", "batch"), axis=0, tiled=True).astype(jnp.float32),
            w_output,
            precision=high,
            preferred_element_type=jnp.float32,
        )
        head_sums = lax.psum_scatter(out_terms, "hidden", scatter_dimension=0, tiled=True)
        share = head_sums.shape[0] // lax.axis_size("batch")
        attended = lax.dynamic_slice_in_dim(head_sums, lax.axis_index("batch") * share, share, 0)
        results.append(attended.astype(jnp.bfloat16))
    return jnp.stack(results)


def split3(value):
    hi = value.astype(BF16)
    rest = value - hi.astype(F32)
    mid = rest.astype(BF16)
    low = (rest - mid.astype(F32)).astype(BF16)
    return hi, mid, low


def project_kernel(
    x_hbm, gain_hbm, wq_hbm, scale_hbm, kw_hbm, vw_hbm, own_ref, *rest
):
    nw = len(rest) - 11
    sends = rest[: nw - 1]
    (
        x_ref, gain_ref, wq_ref, scale_ref, kv_ref, se_ref, so_ref, y_ref, acc_ref, ss_ref, sems,
        block_sems,
    ) = rest[nw - 1 :]
    steps, seqs, depth = x_ref.shape
    rows = steps * seqs
    each = seqs // nw
    blocks, block, words = wq_ref.shape
    groups = se_ref.shape[0]
    per_block = groups // blocks
    group = block // per_block
    b = lax.axis_index("batch")

    def columns(n):
        return pl.ds(pl.multiple_of(b * n, n), n)

    def fetch(i):
        return pltpu.make_async_copy(
            wq_hbm.at[pl.ds(pl.multiple_of(i * block, block), block), columns(words)],
            wq_ref.at[i],
            block_sems.at[i],
        )

    scale_copy = pltpu.make_async_copy(scale_hbm.at[:, columns(2 * words)], scale_ref, sems.at[0])
    others = [
        pltpu.make_async_copy(gain_hbm, gain_ref, sems.at[1]),
        pltpu.make_async_copy(x_hbm, x_ref, sems.at[4]),
    ]
    kvs = [
        pltpu.make_async_copy(kw_hbm.at[:, columns(HEAD)], kv_ref.at[:, :HEAD], sems.at[2]),
        pltpu.make_async_copy(vw_hbm.at[:, columns(HEAD)], kv_ref.at[:, HEAD:], sems.at[3]),
    ]
    scale_copy.start()
    for copy in others:
        copy.start()
    for i in range(3):
        fetch(i).start()

    acc_ref[...] = jnp.zeros_like(acc_ref)
    ss_ref[...] = jnp.zeros_like(ss_ref)
    row = lax.broadcasted_iota(jnp.int32, (256, 256), 0)
    col = lax.broadcasted_iota(jnp.int32, (256, 256), 1)
    pick = jnp.where(row == 2 * (col & 127) + (col >> 7), 1.0, 0.0).astype(BF16)
    scale_copy.wait()
    for c in range(words // 128):
        terms = split3(scale_ref[:, c * 256 : (c + 1) * 256])
        parts = [jnp.dot(term, pick, preferred_element_type=F32) for term in terms]
        both = parts[0] + (parts[1] + parts[2])
        se_ref[:, c * 128 : (c + 1) * 128] = both[:, :128]
        so_ref[:, c * 128 : (c + 1) * 128] = both[:, 128:]
    for copy in others:
        copy.wait()

    chunk = 512

    def step(i, carry):
        here = pl.ds(pl.multiple_of(i * block, block), block)
        x = x_ref[:, :, here].astype(F32)
        x = jnp.concatenate(
            [x[t, v * each : (v + 1) * each] for v in range(nw) for t in range(steps)], axis=0
        )
        y = x * gain_ref[:, here]
        hi = y.astype(BF16)
        low = (y - hi.astype(F32)).astype(BF16)
        lhs = jnp.concatenate([hi, low], axis=0)
        y_ref[i] = lhs
        squares = x * x
        ss_ref[...] += sum(squares[:, c * 128 : (c + 1) * 128] for c in range(block // 128))
        sums = [
            8.0 * jnp.sum(y[:, g * group : (g + 1) * group], axis=1, keepdims=True)
            for g in range(per_block)
        ]
        fetch(i).wait()

        @pl.when(i + 3 < blocks)
        def _():
            fetch(i + 3).start()

        @pl.when(i == 0)
        def _():
            for copy in kvs:
                copy.start()

        for c in range(words // chunk):
            cols = slice(c * chunk, (c + 1) * chunk)
            even = jnp.zeros((rows, chunk), F32)
            odd = jnp.zeros((rows, chunk), F32)
            for g in range(per_block):
                span = slice(g * group, (g + 1) * group)
                word = wq_ref[i, span, cols]
                both = word.astype(F32).astype(BF16)
                upper = (word >> 4).astype(F32).astype(BF16)
                left = lhs[:, span]
                p = jnp.dot(left, both, preferred_element_type=F32)
                u = jnp.dot(left, upper, preferred_element_type=F32)
                p = p[:rows] + p[rows:]
                u = u[:rows] + u[rows:]
                at = pl.ds(i * per_block + g, 1)
                even = even + (p - 16.0 * u - sums[g]) * se_ref[at, cols]
                odd = odd + (u - sums[g]) * so_ref[at, cols]
            acc_ref[:, cols] += even
            acc_ref[:, words + c * chunk : words + (c + 1) * chunk] += odd
        return carry

    def step_kv(i, carry):
        step(i, carry)
        new = jnp.zeros((2 * rows, 2 * HEAD), F32)
        for n in range(2):
            j = 2 * i - blocks + n
            at = pl.ds(pl.multiple_of(j * block, block), block)
            new = new + jnp.dot(y_ref[j], kv_ref[at], preferred_element_type=F32)
        acc_ref[:, 2 * words : 2 * words + 2 * HEAD] += new[:rows] + new[rows:]
        return carry

    lax.fori_loop(0, blocks // 2, step, 0, unroll=4)
    for copy in kvs:
        copy.wait()
    lax.fori_loop(blocks // 2, blocks - 1, step_kv, 0, unroll=3)
    step_kv(blocks - 1, 0)
    lane = lax.broadcasted_iota(jnp.int32, (rows, 128), 1)
    a, m, l = split3(jnp.sum(ss_ref[...], axis=1, keepdims=True))
    a, m, l = a.astype(F32), m.astype(F32), l.astype(F32)
    acc_ref[:, 2 * words + 2 * HEAD :] = jnp.where(
        lane == 0, a, jnp.where(lane == 1, m, jnp.where(lane == 2, l, 0.0))
    )

    me = lax.axis_index("width")
    share = rows // nw

    def piece(s):
        return acc_ref[pl.ds(pl.multiple_of((me ^ s) * share, share), share)]

    own_ref[...] = piece(0)
    for s in range(1, nw):
        sends[s - 1][...] = piece(s).astype(BF16)


def in_hbm(array):
    return pltpu.with_memory_space_constraint(array, pltpu.HBM)


def project(inputs, norm_gain, wq_packed, wq_scales, key_weight, value_weight, nw, nb):
    steps, seqs, depth = inputs.shape
    rows = steps * seqs
    words = wq_packed.shape[1] // nb
    groups = wq_scales.shape[0]
    block = 512
    blocks = depth // block
    cols = 2 * words + 3 * HEAD
    out_rows = rows // nw
    return pl.pallas_call(
        project_kernel,
        in_specs=[HBM] * 6,
        out_specs=[VMEM] * nw,
        out_shape=[jax.ShapeDtypeStruct((out_rows, cols), F32)]
        + [jax.ShapeDtypeStruct((out_rows, cols), BF16)] * (nw - 1),
        scratch_shapes=[
            pltpu.VMEM((steps, seqs, depth), BF16),
            pltpu.VMEM((1, depth), F32),
            pltpu.VMEM((blocks, block, words), jnp.int32),
            pltpu.VMEM((groups, 2 * words), F32),
            pltpu.VMEM((depth, 2 * HEAD), BF16),
            pltpu.VMEM((groups, words), F32),
            pltpu.VMEM((groups, words), F32),
            pltpu.VMEM((blocks, 2 * rows, block), BF16),
            pltpu.VMEM((rows, cols), F32),
            pltpu.VMEM((rows, 128), F32),
            pltpu.SemaphoreType.DMA((5,)),
            pltpu.SemaphoreType.DMA((blocks,)),
        ],
        compiler_params=pltpu.CompilerParams(vmem_limit_bytes=PROJECT_LIMIT),
        name="project",
    )(
        *map(
            in_hbm,
            (inputs, norm_gain.reshape(1, -1), wq_packed, wq_scales, key_weight, value_weight),
        )
    )


def weight_copies(src, dst, start, depth, sems):
    first = lax.axis_index("batch") * depth + start
    count = sems.shape[0]
    each = dst.shape[0] // count
    return [
        pltpu.make_async_copy(
            src.at[pl.ds(pl.multiple_of(first + n * each, each), each)],
            dst.at[pl.ds(n * each, each)],
            sems.at[n],
        )
        for n in range(count)
    ]


def fetch_weight(wo_weight, start, size, depth, after):
    def body(src, after, dst, sems):
        del after
        copies = weight_copies(src, dst, start, depth, sems)
        for copy in copies:
            copy.start()
        for copy in copies:
            copy.wait()

    return pl.pallas_call(
        body,
        in_specs=[HBM, ANY],
        out_specs=VMEM,
        out_shape=pltpu.VMEM((size, wo_weight.shape[1]), BF16),
        scratch_shapes=[pltpu.SemaphoreType.DMA((size // 256,))],
        compiler_params=pltpu.CompilerParams(vmem_limit_bytes=FETCH_LIMIT),
        name="fetch",
    )(in_hbm(wo_weight), after)


def attend_kernel(heads, nw, start, len_ref, own_ref, *rest):
    parts = rest[: nw - 1]
    (
        cq_ref, sq_ref, ck_ref, sk_ref, k_own, k_mate, v_own, v_mate, wo_hbm, _, out_ref, wo_ref, k_buf, v_buf, q_ref,
        m_ref, sems, wo_sems,
    ) = rest[nw - 1 :]
    held, slots, _ = k_own.shape
    b = lax.axis_index("batch")
    column = pl.ds(pl.multiple_of(b * HEAD, HEAD), HEAD)
    copies = [
        pltpu.make_async_copy(
            src.at[:, :, column], buf.at[pl.ds(place * held, held)], sems.at[n]
        )
        for n, (src, buf, place) in enumerate(
            ((k_own, k_buf, b), (k_mate, k_buf, 1 - b), (v_own, v_buf, b), (v_mate, v_buf, 1 - b))
        )
    ]
    incoming = weight_copies(wo_hbm, wo_ref, start, heads * HEAD, wo_sems)
    for copy in copies + incoming:
        copy.start()

    rows = own_ref.shape[0]
    seqs = rows // STEPS
    half = heads * HEAD // 2
    total = own_ref[...]
    for part in parts:
        total = total + part[...].astype(F32)
    squares = jnp.sum(total[:, 2 * half + 2 * HEAD :], axis=1, keepdims=True)
    total = total * lax.rsqrt(squares / D + EPS)

    lane = lax.broadcasted_iota(jnp.int32, (rows, HEAD), 1)
    left = lane < HEAD // 2
    tiles = []
    for m in range(heads // 2):
        e = total[:, m * HEAD : (m + 1) * HEAD]
        o = total[:, half + m * HEAD : half + (m + 1) * HEAD]
        tiles.append(jnp.where(left, e, pltpu.roll(o, HEAD // 2, 1)))
        tiles.append(jnp.where(left, pltpu.roll(e, HEAD // 2, 1), o))
    cos_q, sin_q, cos_k, sin_k = cq_ref[...], sq_ref[...], ck_ref[...], sk_ref[...]
    near = (lane & (HEAD // 2 - 1)) < HEAD // 4
    turned = []
    for q in tiles:
        other = jnp.where(near, pltpu.roll(q, HEAD - HEAD // 4, 1), pltpu.roll(q, HEAD // 4, 1))
        turned.append(q * cos_q + other * sin_q)
    q_all = jnp.concatenate(turned, axis=0).astype(BF16)
    row = lax.broadcasted_iota(jnp.int32, (HEAD, HEAD), 0)
    col = lax.broadcasted_iota(jnp.int32, (HEAD, HEAD), 1)
    order = jnp.where(col == 2 * (row & (HEAD // 2 - 1)) + row // (HEAD // 2), 1.0, 0.0).astype(BF16)
    q_ref[...] = jnp.dot(q_all, order, preferred_element_type=F32)
    k_new = total[:, 2 * half : 2 * half + HEAD]
    k_new = (k_new * cos_k + pltpu.roll(k_new, HEAD // 2, 1) * sin_k).astype(BF16).astype(F32)
    v_new = total[:, 2 * half + HEAD : 2 * half + 2 * HEAD].astype(BF16).astype(F32)

    for copy in copies:
        copy.wait()

    each = STEPS * heads
    queries = [
        jnp.concatenate(
            [q_ref[pl.ds(t * seqs + j, heads, stride=rows), :] for t in range(STEPS)], axis=0
        )
        for j in range(seqs)
    ]
    scores = jnp.concatenate(
        [
            lax.dot_general(
                queries[j].astype(BF16), k_buf[j], (((1,), (1,)), ((), ())),
                preferred_element_type=F32,
            )
            for j in range(seqs)
        ],
        axis=0,
    ) * HEAD ** (-0.5)
    row = lax.broadcasted_iota(jnp.int32, (seqs * each, 1), 0)
    filled = jnp.full((seqs * each, 1), len_ref[seqs - 1], jnp.int32)
    for j in range(seqs - 1, 0, -1):
        filled = jnp.where(row < j * each, len_ref[j - 1], filled)
    slot = lax.broadcasted_iota(jnp.int32, (seqs * each, slots), 1)
    scores = jnp.where(slot < filled, scores, -1e30)

    def fresh(t):
        dots = [
            jnp.sum(queries[j] * k_new[t * seqs + j : t * seqs + j + 1], axis=1, keepdims=True)
            for j in range(seqs)
        ]
        return jnp.concatenate(dots, axis=0) * HEAD ** (-0.5)

    first = fresh(0)
    second = jnp.where(lax.rem(row, each) >= heads, fresh(1), -1e30)
    peak = jnp.maximum(jnp.max(scores, axis=1, keepdims=True), jnp.maximum(first, second))
    weights = jnp.exp(scores - peak)
    first = jnp.exp(first - peak)
    second = jnp.exp(second - peak)
    inverse = 1.0 / (jnp.sum(weights, axis=1, keepdims=True) + first + second)
    probs = (weights * inverse).astype(BF16)
    first = (first * inverse).astype(BF16).astype(F32)
    second = (second * inverse).astype(BF16).astype(F32)
    for j in range(seqs):
        span = slice(j * each, (j + 1) * each)
        mixed = jnp.dot(probs[span], v_buf[j], preferred_element_type=F32)
        mixed = mixed + first[span] * v_new[j : j + 1]
        mixed = mixed + second[span] * v_new[seqs + j : seqs + j + 1]
        for t in range(STEPS):
            m_ref[pl.ds(t * seqs + j, heads, stride=rows), :] = mixed[t * heads : (t + 1) * heads]
    for n in range(heads):
        out_ref[:, n * HEAD : (n + 1) * HEAD] = m_ref[n * rows : (n + 1) * rows, :].astype(BF16)
    for copy in incoming:
        copy.wait()


def attend(own, parts, table, lengths, k_own, k_mate, v_own, v_mate, wo_weight, start, size, after, heads):
    rows = own.shape[0]
    each, slots, _ = k_own.shape
    nw = len(parts) + 1
    body = lambda *refs: attend_kernel(heads, nw, start, *refs)
    return pl.pallas_call(
        body,
        in_specs=[pl.BlockSpec(memory_space=pltpu.SMEM)] + [VMEM] * (nw + 4) + [ANY] * 4 + [HBM, ANY],
        out_specs=[VMEM, VMEM],
        out_shape=[
            jax.ShapeDtypeStruct((rows, heads * HEAD), BF16),
            pltpu.VMEM((size, wo_weight.shape[1]), BF16),
        ],
        scratch_shapes=[
            pltpu.VMEM((2 * each, slots, HEAD), BF16),
            pltpu.VMEM((2 * each, slots, HEAD), BF16),
            pltpu.VMEM((heads * rows, HEAD), F32),
            pltpu.VMEM((heads * rows, HEAD), F32),
            pltpu.SemaphoreType.DMA((4,)),
            pltpu.SemaphoreType.DMA((size // 256,)),
        ],
        compiler_params=pltpu.CompilerParams(vmem_limit_bytes=ATTEND_LIMIT),

        name="attend",
    )(lengths, own, *parts, *table, in_hbm(k_own), k_mate, in_hbm(v_own), v_mate, in_hbm(wo_weight), after)


def output_kernel(nw, count, *refs):
    pieces = refs[:nw]
    weights = refs[nw : nw + count]
    outs = refs[nw + count : 2 * nw + count]
    piece_ref, acc_ref = refs[2 * nw + count :]
    rows, depth = pieces[0].shape
    cols = weights[0].shape[1]
    place = lax.axis_index("width")
    for s in range(nw):
        piece_ref[place ^ s] = pieces[s][...].astype(F32)
    lhs = piece_ref[...].reshape(nw * rows, depth).astype(BF16)
    block = 512
    for n in range(cols // block):
        span = slice(n * block, (n + 1) * block)
        acc = jnp.zeros((nw * rows, block), F32)
        first = 0
        for w_ref in weights:
            last = first + w_ref.shape[0]
            acc = acc + jnp.dot(lhs[:, first:last], w_ref[:, span], preferred_element_type=F32)
            first = last
        acc_ref[:, :, span] = acc.reshape(nw, rows, block)
    me = lax.axis_index("hidden") * lax.axis_size("batch") + lax.axis_index("batch")
    for s in range(nw):
        value = acc_ref[me ^ s].astype(outs[s].dtype)
        for t in range(STEPS):
            outs[s][t] = value[t * rows // STEPS : (t + 1) * rows // STEPS]


def output(pieces, weights):
    nw, count = len(pieces), len(weights)
    rows, depth = pieces[0].shape
    cols = weights[0].shape[1]
    body = lambda *refs: output_kernel(nw, count, *refs)
    shape = (STEPS, rows // STEPS, cols)
    return pl.pallas_call(
        body,
        in_specs=[VMEM] * (nw + count),
        out_specs=[VMEM] * nw,
        out_shape=[jax.ShapeDtypeStruct(shape, dtype) for dtype in (F32, BF16, F32, BF16)],
        scratch_shapes=[
            pltpu.VMEM((nw, rows, depth), F32),
            pltpu.VMEM((nw, rows, cols), F32),
        ],
        compiler_params=pltpu.CompilerParams(vmem_limit_bytes=OUTPUT_LIMIT),
        name="output",
    )(*pieces, *weights)


def rotary_tables(positions):
    lane = jnp.arange(HEAD, dtype=jnp.int32)
    parity = 2 * (lane % (HEAD // 2)) + lane // (HEAD // 2)
    out = []
    for dim in (parity, lane):
        pair = (dim % (HEAD // 2)).astype(F32)
        freq = 500000.0 ** (-2.0 * pair / HEAD)
        angle = positions.astype(F32)[:, None] * freq[None, :]
        sign = jnp.where(dim < HEAD // 2, -1.0, 1.0)[None, :]
        out += [jnp.cos(angle), jnp.sin(angle) * sign]
    return out


def split_heads(
    inputs,
    norm_gain,
    wq_packed,
    wq_scales,
    key_weight,
    value_weight,
    wo_weight,
    key_cache,
    value_cache,
    lengths,
):
    nw, nh, nb = lax.axis_size("width"), lax.axis_size("hidden"), lax.axis_size("batch")
    swap = [(0, 1), (1, 0)]
    k_mate = lax.ppermute(key_cache, "batch", swap)
    v_mate = lax.ppermute(value_cache, "batch", swap)
    len_mate = lax.ppermute(lengths, "batch", swap)

    own, *sends = project(
        inputs, norm_gain, wq_packed, wq_scales, key_weight, value_weight, nw, nb
    )
    own, k_mate, v_mate, len_mate, *sends = lax.optimization_barrier(
        (own, k_mate, v_mate, len_mate, *sends)
    )
    first = lax.axis_index("batch") == 0
    len_all = jnp.where(
        first, jnp.concatenate([lengths, len_mate]), jnp.concatenate([len_mate, lengths])
    )
    positions = jnp.concatenate([len_all + step for step in range(STEPS)])
    table = rotary_tables(positions)
    parts = [
        lax.ppermute(piece, "width", [(i, i ^ s) for i in range(nw)])
        for s, piece in enumerate(sends, 1)
    ]
    heads = 2 * wq_packed.shape[1] // nb // HEAD
    depth = heads * HEAD
    early, middle, late = EARLY * depth // 8, MIDDLE * depth // 8, LATE * depth // 8
    w_early = fetch_weight(wo_weight, 0, early, depth, own)
    mixed, w_middle = attend(
        own, parts[::-1], table, len_all, key_cache, k_mate, value_cache, v_mate, wo_weight, early, middle,
        w_early, heads,
    )
    w_late = fetch_weight(wo_weight, early + middle, late, depth, mixed)
    pieces = [mixed] + [
        lax.ppermute(mixed, "width", [(i, i ^ s) for i in range(nw)]) for s in range(1, nw)
    ]
    here, across_core, across_chip, across_both = output(pieces, [w_early, w_middle, w_late])
    relay = lax.ppermute(across_both, "batch", swap)
    near = lax.ppermute(across_core, "batch", swap)
    leaving = (across_chip + relay.astype(F32)).astype(BF16)
    far = lax.ppermute(leaving, "hidden", swap)
    sums = here + near.astype(F32) + far.astype(F32)
    return sums.astype(BF16)


def solution(mesh):
    sizes = mesh.shape

    def on_device(*args):
        kv_local = args[4].shape[1] // HEAD
        fits = (
            sizes["batch"] == 2
            and sizes["hidden"] == 2
            and kv_local == 2
            and sizes["width"] == sizes["hidden"] * sizes["batch"]
            and args[0].shape[1] // sizes["width"] == 2 * args[9].shape[0]
            and args[0].shape[2] % 512 == 0
            and STEPS * args[0].shape[1] // sizes["width"] % 8 == 0
        )
        return split_heads(*args) if fits else general(*args)

    in_specs = (
        P(None, "groups", "width"),
        P("width"),
        P("width", "hidden"),
        P("width", "hidden"),
        P("width", "hidden"),
        P("width", "hidden"),
        P("hidden", "width"),
        P(("groups", "width", "batch"), None, "hidden"),
        P(("groups", "width", "batch"), None, "hidden"),
        P(("groups", "width", "batch")),
    )
    out_specs = P(None, ("groups", "hidden", "batch"), "width")
    return jax.shard_map(
        on_device, mesh=mesh, in_specs=in_specs, out_specs=out_specs, check_vma=False
    )
```

```python
import jax
import jax.numpy as jnp
from jax import lax
from jax.experimental import pallas as pl
from jax.experimental.pallas import tpu as pltpu
from jax.sharding import PartitionSpec as P

D = 16384
HEAD = 128
STEPS = 2
EPS = 1e-05
BF16 = jnp.bfloat16
F32 = jnp.float32
MIB = 1024 * 1024
PROJECT_LIMIT = 26 * MIB
ATTEND_LIMIT = 10 * MIB
OUTPUT_LIMIT = 10 * MIB
FETCH_LIMIT = 1 * MIB
EARLY, MIDDLE, LATE = 2, 3, 3
HBM = pl.BlockSpec(memory_space=pltpu.HBM)
ANY = pl.BlockSpec(memory_space=pl.ANY)
VMEM = pl.BlockSpec(memory_space=pltpu.VMEM)


def unpack_weights(packed, scales, bits, per_word):
    shifts = jnp.arange(per_word, dtype=jnp.int32) * bits
    codes = packed[:, :, None] >> shifts & (1 << bits) - 1
    values = (codes - (1 << bits - 1)).astype(jnp.float32)
    values = values.reshape(packed.shape[0], packed.shape[1] * per_word)
    group_rows = packed.shape[0] // scales.shape[0]
    values = values.reshape(scales.shape[0], group_rows, values.shape[1]) * scales[:, None, :]
    return values.reshape(packed.shape[0], -1)


def rotate_heads(field, positions):
    half = field.shape[-1] // 2
    freq = 500000.0 ** (-2.0 * jnp.arange(half, dtype=jnp.float32) / field.shape[-1])
    angle = positions.astype(jnp.float32)[:, None] * freq[None, :]
    cosine = jnp.cos(angle)[:, None, :]
    sine = jnp.sin(angle)[:, None, :]
    first = field[..., :half]
    second = field[..., half:]
    return jnp.concatenate(
        [first * cosine - second * sine, second * cosine + first * sine], axis=-1
    )


def general(
    inputs,
    norm_gain,
    wq_packed,
    wq_scales,
    key_weight,
    value_weight,
    wo_weight,
    key_cache,
    value_cache,
    lengths,
):
    high = lax.Precision.HIGHEST
    w_query = unpack_weights(wq_packed, wq_scales, 4, 2)
    w_output = wo_weight.astype(jnp.float32)
    w_joined = jnp.concatenate(
        [w_query, key_weight.astype(jnp.float32), value_weight.astype(jnp.float32)], axis=1
    )
    seq_local = lengths.shape[0]
    slots = key_cache.shape[1]
    kv_local = key_weight.shape[1] // HEAD
    q_local = w_query.shape[1] // HEAD
    repeat = q_local // kv_local
    cols_local = inputs.shape[2]
    keys_all = key_cache
    values_all = value_cache
    slot_ids = jnp.arange(slots, dtype=jnp.int32)
    results = []
    for step in range(STEPS):
        rows = inputs[step].astype(jnp.float32)
        width_count = lax.axis_size("width")
        batch_count = lax.axis_size("batch")
        arranged = rows.reshape(width_count, batch_count, seq_local, cols_local)
        rows = lax.dynamic_index_in_dim(arranged, lax.axis_index("batch"), 1, keepdims=False)
        rows = rows.reshape(width_count * seq_local, cols_local)
        squares = jnp.sum(rows * rows, axis=1)
        total = lax.psum(squares, "width")
        scale = lax.rsqrt(total / D + EPS)
        normed = rows * scale[:, None] * norm_gain[None, :]
        partial_value = jnp.dot(
            normed, w_joined, precision=high, preferred_element_type=jnp.float32
        )
        projected = lax.psum_scatter(partial_value, "width", scatter_dimension=0, tiled=True)
        positions = lengths + step
        q_cols = q_local * HEAD
        kv_cols = kv_local * HEAD
        queries = rotate_heads(
            projected[:, :q_cols].reshape(seq_local, q_local, HEAD), positions
        ).astype(jnp.bfloat16)
        keys_new = rotate_heads(
            projected[:, q_cols : q_cols + kv_cols].reshape(seq_local, kv_local, HEAD), positions
        )
        keys_new = keys_new.reshape(seq_local, kv_cols).astype(jnp.bfloat16)
        values_new = projected[:, q_cols + kv_cols :].astype(jnp.bfloat16)
        written = slot_ids[None, :, None] == positions[:, None, None]
        keys_all = jnp.where(written, keys_new[:, None, :], keys_all)
        values_all = jnp.where(written, values_new[:, None, :], values_all)
        query_heads = queries.reshape(seq_local, kv_local, repeat, HEAD)
        key_heads = keys_all.reshape(seq_local, slots, kv_local, HEAD)
        value_heads = values_all.reshape(seq_local, slots, kv_local, HEAD)
        scores = jnp.einsum(
            "bgrd,bsgd->bgrs", query_heads, key_heads, preferred_element_type=jnp.float32
        ) * HEAD ** (-0.5)
        valid = slot_ids[None, None, None, :] <= positions[:, None, None, None]
        scores = jnp.where(valid, scores, -1e30)
        peak = jnp.max(scores, axis=-1, keepdims=True)
        weights = jnp.exp(scores - peak)
        total_weight = jnp.sum(weights, axis=-1, keepdims=True)
        probs = (weights / total_weight).astype(jnp.bfloat16)
        mixed = jnp.einsum(
            "bgrs,bsgd->bgrd", probs, value_heads, preferred_element_type=jnp.float32
        )
        mixed = mixed.reshape(seq_local, q_cols).astype(jnp.bfloat16)
        out_terms = jnp.dot(
            lax.all_gather(mixed, ("width", "batch"), axis=0, tiled=True).astype(jnp.float32),
            w_output,
            precision=high,
            preferred_element_type=jnp.float32,
        )
        head_sums = lax.psum_scatter(out_terms, "hidden", scatter_dimension=0, tiled=True)
        share = head_sums.shape[0] // lax.axis_size("batch")
        attended = lax.dynamic_slice_in_dim(head_sums, lax.axis_index("batch") * share, share, 0)
        results.append(attended.astype(jnp.bfloat16))
    return jnp.stack(results)


def split3(value):
    hi = value.astype(BF16)
    rest = value - hi.astype(F32)
    mid = rest.astype(BF16)
    low = (rest - mid.astype(F32)).astype(BF16)
    return hi, mid, low


def project_kernel(
    x_hbm, gain_hbm, wq_hbm, scale_hbm, kw_hbm, vw_hbm, own_ref, *rest
):
    nw = len(rest) - 11
    sends = rest[: nw - 1]
    (
        x_ref, gain_ref, wq_ref, scale_ref, kv_ref, se_ref, so_ref, y_ref, acc_ref, ss_ref, sems,
        block_sems,
    ) = rest[nw - 1 :]
    steps, seqs, depth = x_ref.shape
    rows = steps * seqs
    each = seqs // nw
    blocks, block, words = wq_ref.shape
    groups = se_ref.shape[0]
    per_block = groups // blocks
    group = block // per_block
    b = lax.axis_index("batch")

    def columns(n):
        return pl.ds(pl.multiple_of(b * n, n), n)

    def fetch(i):
        return pltpu.make_async_copy(
            wq_hbm.at[pl.ds(pl.multiple_of(i * block, block), block), columns(words)],
            wq_ref.at[i],
            block_sems.at[i],
        )

    scale_copy = pltpu.make_async_copy(scale_hbm.at[:, columns(2 * words)], scale_ref, sems.at[0])
    others = [
        pltpu.make_async_copy(gain_hbm, gain_ref, sems.at[1]),
        pltpu.make_async_copy(x_hbm, x_ref, sems.at[4]),
    ]
    kvs = [
        pltpu.make_async_copy(kw_hbm.at[:, columns(HEAD)], kv_ref.at[:, :HEAD], sems.at[2]),
        pltpu.make_async_copy(vw_hbm.at[:, columns(HEAD)], kv_ref.at[:, HEAD:], sems.at[3]),
    ]
    scale_copy.start()
    for copy in others:
        copy.start()
    for i in range(3):
        fetch(i).start()

    acc_ref[...] = jnp.zeros_like(acc_ref)
    ss_ref[...] = jnp.zeros_like(ss_ref)
    row = lax.broadcasted_iota(jnp.int32, (256, 256), 0)
    col = lax.broadcasted_iota(jnp.int32, (256, 256), 1)
    pick = jnp.where(row == 2 * (col & 127) + (col >> 7), 1.0, 0.0).astype(BF16)
    scale_copy.wait()
    for c in range(words // 128):
        terms = split3(scale_ref[:, c * 256 : (c + 1) * 256])
        parts = [jnp.dot(term, pick, preferred_element_type=F32) for term in terms]
        both = parts[0] + (parts[1] + parts[2])
        se_ref[:, c * 128 : (c + 1) * 128] = both[:, :128]
        so_ref[:, c * 128 : (c + 1) * 128] = both[:, 128:]
    for copy in others:
        copy.wait()

    chunk = 512

    def step(i, carry):
        here = pl.ds(pl.multiple_of(i * block, block), block)
        x = x_ref[:, :, here].astype(F32)
        x = jnp.concatenate(
            [x[t, v * each : (v + 1) * each] for v in range(nw) for t in range(steps)], axis=0
        )
        y = x * gain_ref[:, here]
        hi = y.astype(BF16)
        low = (y - hi.astype(F32)).astype(BF16)
        lhs = jnp.concatenate([hi, low], axis=0)
        y_ref[i] = lhs
        squares = x * x
        ss_ref[...] += sum(squares[:, c * 128 : (c + 1) * 128] for c in range(block // 128))
        sums = [
            8.0 * jnp.sum(y[:, g * group : (g + 1) * group], axis=1, keepdims=True)
            for g in range(per_block)
        ]
        fetch(i).wait()

        @pl.when(i + 3 < blocks)
        def _():
            fetch(i + 3).start()

        @pl.when(i == 0)
        def _():
            for copy in kvs:
                copy.start()

        for c in range(words // chunk):
            cols = slice(c * chunk, (c + 1) * chunk)
            even = jnp.zeros((rows, chunk), F32)
            odd = jnp.zeros((rows, chunk), F32)
            for g in range(per_block):
                span = slice(g * group, (g + 1) * group)
                word = wq_ref[i, span, cols]
                both = word.astype(F32).astype(BF16)
                upper = (word >> 4).astype(F32).astype(BF16)
                left = lhs[:, span]
                p = jnp.dot(left, both, preferred_element_type=F32)
                u = jnp.dot(left, upper, preferred_element_type=F32)
                p = p[:rows] + p[rows:]
                u = u[:rows] + u[rows:]
                at = pl.ds(i * per_block + g, 1)
                even = even + (p - 16.0 * u - sums[g]) * se_ref[at, cols]
                odd = odd + (u - sums[g]) * so_ref[at, cols]
            acc_ref[:, cols] += even
            acc_ref[:, words + c * chunk : words + (c + 1) * chunk] += odd
        return carry

    def step_kv(i, carry):
        step(i, carry)
        new = jnp.zeros((2 * rows, 2 * HEAD), F32)
        for n in range(2):
            j = 2 * i - blocks + n
            at = pl.ds(pl.multiple_of(j * block, block), block)
            new = new + jnp.dot(y_ref[j], kv_ref[at], preferred_element_type=F32)
        acc_ref[:, 2 * words : 2 * words + 2 * HEAD] += new[:rows] + new[rows:]
        return carry

    lax.fori_loop(0, blocks // 2, step, 0, unroll=4)
    for copy in kvs:
        copy.wait()
    lax.fori_loop(blocks // 2, blocks - 1, step_kv, 0, unroll=3)
    step_kv(blocks - 1, 0)
    lane = lax.broadcasted_iota(jnp.int32, (rows, 128), 1)
    a, m, l = split3(jnp.sum(ss_ref[...], axis=1, keepdims=True))
    a, m, l = a.astype(F32), m.astype(F32), l.astype(F32)
    acc_ref[:, 2 * words + 2 * HEAD :] = jnp.where(
        lane == 0, a, jnp.where(lane == 1, m, jnp.where(lane == 2, l, 0.0))
    )

    me = lax.axis_index("width")
    share = rows // nw

    def piece(s):
        return acc_ref[pl.ds(pl.multiple_of((me ^ s) * share, share), share)]

    own_ref[...] = piece(0)
    for s in range(1, nw):
        sends[s - 1][...] = piece(s).astype(BF16)


def in_hbm(array):
    return pltpu.with_memory_space_constraint(array, pltpu.HBM)


def project(inputs, norm_gain, wq_packed, wq_scales, key_weight, value_weight, nw, nb):
    steps, seqs, depth = inputs.shape
    rows = steps * seqs
    words = wq_packed.shape[1] // nb
    groups = wq_scales.shape[0]
    block = 512
    blocks = depth // block
    cols = 2 * words + 3 * HEAD
    out_rows = rows // nw
    return pl.pallas_call(
        project_kernel,
        in_specs=[HBM] * 6,
        out_specs=[VMEM] * nw,
        out_shape=[jax.ShapeDtypeStruct((out_rows, cols), F32)]
        + [jax.ShapeDtypeStruct((out_rows, cols), BF16)] * (nw - 1),
        scratch_shapes=[
            pltpu.VMEM((steps, seqs, depth), BF16),
            pltpu.VMEM((1, depth), F32),
            pltpu.VMEM((blocks, block, words), jnp.int32),
            pltpu.VMEM((groups, 2 * words), F32),
            pltpu.VMEM((depth, 2 * HEAD), BF16),
            pltpu.VMEM((groups, words), F32),
            pltpu.VMEM((groups, words), F32),
            pltpu.VMEM((blocks, 2 * rows, block), BF16),
            pltpu.VMEM((rows, cols), F32),
            pltpu.VMEM((rows, 128), F32),
            pltpu.SemaphoreType.DMA((5,)),
            pltpu.SemaphoreType.DMA((blocks,)),
        ],
        compiler_params=pltpu.CompilerParams(vmem_limit_bytes=PROJECT_LIMIT),
        name="project",
    )(
        *map(
            in_hbm,
            (inputs, norm_gain.reshape(1, -1), wq_packed, wq_scales, key_weight, value_weight),
        )
    )


def weight_copies(src, dst, start, depth, sems):
    first = lax.axis_index("batch") * depth + start
    count = sems.shape[0]
    each = dst.shape[0] // count
    return [
        pltpu.make_async_copy(
            src.at[pl.ds(pl.multiple_of(first + n * each, each), each)],
            dst.at[pl.ds(n * each, each)],
            sems.at[n],
        )
        for n in range(count)
    ]


def fetch_weight(wo_weight, start, size, depth, after):
    def body(src, after, dst, sems):
        del after
        copies = weight_copies(src, dst, start, depth, sems)
        for copy in copies:
            copy.start()
        for copy in copies:
            copy.wait()

    return pl.pallas_call(
        body,
        in_specs=[HBM, ANY],
        out_specs=VMEM,
        out_shape=pltpu.VMEM((size, wo_weight.shape[1]), BF16),
        scratch_shapes=[pltpu.SemaphoreType.DMA((size // 256,))],
        compiler_params=pltpu.CompilerParams(vmem_limit_bytes=FETCH_LIMIT),
        name="fetch",
    )(in_hbm(wo_weight), after)


def attend_kernel(heads, nw, start, len_ref, own_ref, *rest):
    parts = rest[: nw - 1]
    (
        cq_ref, sq_ref, ck_ref, sk_ref, k_own, k_mate, v_own, v_mate, wo_hbm, _, out_ref, wo_ref, k_buf, v_buf, q_ref,
        m_ref, sems, wo_sems,
    ) = rest[nw - 1 :]
    held, slots, _ = k_own.shape
    b = lax.axis_index("batch")
    column = pl.ds(pl.multiple_of(b * HEAD, HEAD), HEAD)
    copies = [
        pltpu.make_async_copy(
            src.at[:, :, column], buf.at[pl.ds(place * held, held)], sems.at[n]
        )
        for n, (src, buf, place) in enumerate(
            ((k_own, k_buf, b), (k_mate, k_buf, 1 - b), (v_own, v_buf, b), (v_mate, v_buf, 1 - b))
        )
    ]
    incoming = weight_copies(wo_hbm, wo_ref, start, heads * HEAD, wo_sems)
    for copy in copies + incoming:
        copy.start()

    rows = own_ref.shape[0]
    seqs = rows // STEPS
    half = heads * HEAD // 2
    total = own_ref[...]
    for part in parts:
        total = total + part[...].astype(F32)
    squares = jnp.sum(total[:, 2 * half + 2 * HEAD :], axis=1, keepdims=True)
    total = total * lax.rsqrt(squares / D + EPS)

    lane = lax.broadcasted_iota(jnp.int32, (rows, HEAD), 1)
    left = lane < HEAD // 2
    tiles = []
    for m in range(heads // 2):
        e = total[:, m * HEAD : (m + 1) * HEAD]
        o = total[:, half + m * HEAD : half + (m + 1) * HEAD]
        tiles.append(jnp.where(left, e, pltpu.roll(o, HEAD // 2, 1)))
        tiles.append(jnp.where(left, pltpu.roll(e, HEAD // 2, 1), o))
    cos_q, sin_q, cos_k, sin_k = cq_ref[...], sq_ref[...], ck_ref[...], sk_ref[...]
    near = (lane & (HEAD // 2 - 1)) < HEAD // 4
    turned = []
    for q in tiles:
        other = jnp.where(near, pltpu.roll(q, HEAD - HEAD // 4, 1), pltpu.roll(q, HEAD // 4, 1))
        turned.append(q * cos_q + other * sin_q)
    q_all = jnp.concatenate(turned, axis=0).astype(BF16)
    row = lax.broadcasted_iota(jnp.int32, (HEAD, HEAD), 0)
    col = lax.broadcasted_iota(jnp.int32, (HEAD, HEAD), 1)
    order = jnp.where(col == 2 * (row & (HEAD // 2 - 1)) + row // (HEAD // 2), 1.0, 0.0).astype(BF16)
    q_ref[...] = jnp.dot(q_all, order, preferred_element_type=F32)
    k_new = total[:, 2 * half : 2 * half + HEAD]
    k_new = (k_new * cos_k + pltpu.roll(k_new, HEAD // 2, 1) * sin_k).astype(BF16).astype(F32)
    v_new = total[:, 2 * half + HEAD : 2 * half + 2 * HEAD].astype(BF16).astype(F32)

    for copy in copies:
        copy.wait()

    each = STEPS * heads
    queries = [
        jnp.concatenate(
            [q_ref[pl.ds(t * seqs + j, heads, stride=rows), :] for t in range(STEPS)], axis=0
        )
        for j in range(seqs)
    ]
    scores = jnp.concatenate(
        [
            lax.dot_general(
                queries[j].astype(BF16), k_buf[j], (((1,), (1,)), ((), ())),
                preferred_element_type=F32,
            )
            for j in range(seqs)
        ],
        axis=0,
    ) * HEAD ** (-0.5)
    row = lax.broadcasted_iota(jnp.int32, (seqs * each, 1), 0)
    filled = jnp.full((seqs * each, 1), len_ref[seqs - 1], jnp.int32)
    for j in range(seqs - 1, 0, -1):
        filled = jnp.where(row < j * each, len_ref[j - 1], filled)
    slot = lax.broadcasted_iota(jnp.int32, (seqs * each, slots), 1)
    scores = jnp.where(slot < filled, scores, -1e30)

    def fresh(t):
        dots = [
            jnp.sum(queries[j] * k_new[t * seqs + j : t * seqs + j + 1], axis=1, keepdims=True)
            for j in range(seqs)
        ]
        return jnp.concatenate(dots, axis=0) * HEAD ** (-0.5)

    first = fresh(0)
    second = jnp.where(lax.rem(row, each) >= heads, fresh(1), -1e30)
    peak = jnp.maximum(jnp.max(scores, axis=1, keepdims=True), jnp.maximum(first, second))
    weights = jnp.exp(scores - peak)
    first = jnp.exp(first - peak)
    second = jnp.exp(second - peak)
    inverse = 1.0 / (jnp.sum(weights, axis=1, keepdims=True) + first + second)
    probs = (weights * inverse).astype(BF16)
    first = (first * inverse).astype(BF16).astype(F32)
    second = (second * inverse).astype(BF16).astype(F32)
    for j in range(seqs):
        span = slice(j * each, (j + 1) * each)
        mixed = jnp.dot(probs[span], v_buf[j], preferred_element_type=F32)
        mixed = mixed + first[span] * v_new[j : j + 1]
        mixed = mixed + second[span] * v_new[seqs + j : seqs + j + 1]
        for t in range(STEPS):
            m_ref[pl.ds(t * seqs + j, heads, stride=rows), :] = mixed[t * heads : (t + 1) * heads]
    for n in range(heads):
        out_ref[:, n * HEAD : (n + 1) * HEAD] = m_ref[n * rows : (n + 1) * rows, :].astype(BF16)
    for copy in incoming:
        copy.wait()


def attend(own, parts, table, lengths, k_own, k_mate, v_own, v_mate, wo_weight, start, size, after, heads):
    rows = own.shape[0]
    each, slots, _ = k_own.shape
    nw = len(parts) + 1
    body = lambda *refs: attend_kernel(heads, nw, start, *refs)
    return pl.pallas_call(
        body,
        in_specs=[pl.BlockSpec(memory_space=pltpu.SMEM)] + [VMEM] * (nw + 4) + [ANY] * 4 + [HBM, ANY],
        out_specs=[VMEM, VMEM],
        out_shape=[
            jax.ShapeDtypeStruct((rows, heads * HEAD), BF16),
            pltpu.VMEM((size, wo_weight.shape[1]), BF16),
        ],
        scratch_shapes=[
            pltpu.VMEM((2 * each, slots, HEAD), BF16),
            pltpu.VMEM((2 * each, slots, HEAD), BF16),
            pltpu.VMEM((heads * rows, HEAD), F32),
            pltpu.VMEM((heads * rows, HEAD), F32),
            pltpu.SemaphoreType.DMA((4,)),
            pltpu.SemaphoreType.DMA((size // 256,)),
        ],
        compiler_params=pltpu.CompilerParams(vmem_limit_bytes=ATTEND_LIMIT),

        name="attend",
    )(lengths, own, *parts, *table, in_hbm(k_own), k_mate, in_hbm(v_own), v_mate, in_hbm(wo_weight), after)


def output_kernel(nw, count, *refs):
    pieces = refs[:nw]
    weights = refs[nw : nw + count]
    outs = refs[nw + count : 2 * nw + count]
    piece_ref, acc_ref = refs[2 * nw + count :]
    rows, depth = pieces[0].shape
    cols = weights[0].shape[1]
    place = lax.axis_index("width")
    for s in range(nw):
        piece_ref[place ^ s] = pieces[s][...].astype(F32)
    lhs = piece_ref[...].reshape(nw * rows, depth).astype(BF16)
    block = 512
    for n in range(cols // block):
        span = slice(n * block, (n + 1) * block)
        acc = jnp.zeros((nw * rows, block), F32)
        first = 0
        for w_ref in weights:
            last = first + w_ref.shape[0]
            acc = acc + jnp.dot(lhs[:, first:last], w_ref[:, span], preferred_element_type=F32)
            first = last
        acc_ref[:, :, span] = acc.reshape(nw, rows, block)
    me = lax.axis_index("hidden") * lax.axis_size("batch") + lax.axis_index("batch")
    for s in range(nw):
        value = acc_ref[me ^ s].astype(outs[s].dtype)
        for t in range(STEPS):
            outs[s][t] = value[t * rows // STEPS : (t + 1) * rows // STEPS]


def output(pieces, weights):
    nw, count = len(pieces), len(weights)
    rows, depth = pieces[0].shape
    cols = weights[0].shape[1]
    body = lambda *refs: output_kernel(nw, count, *refs)
    shape = (STEPS, rows // STEPS, cols)
    return pl.pallas_call(
        body,
        in_specs=[VMEM] * (nw + count),
        out_specs=[VMEM] * nw,
        out_shape=[jax.ShapeDtypeStruct(shape, dtype) for dtype in (F32, BF16, F32, BF16)],
        scratch_shapes=[
            pltpu.VMEM((nw, rows, depth), F32),
            pltpu.VMEM((nw, rows, cols), F32),
        ],
        compiler_params=pltpu.CompilerParams(vmem_limit_bytes=OUTPUT_LIMIT),
        name="output",
    )(*pieces, *weights)


def rotary_tables(positions):
    lane = jnp.arange(HEAD, dtype=jnp.int32)
    parity = 2 * (lane % (HEAD // 2)) + lane // (HEAD // 2)
    out = []
    for dim in (parity, lane):
        pair = (dim % (HEAD // 2)).astype(F32)
        freq = 500000.0 ** (-2.0 * pair / HEAD)
        angle = positions.astype(F32)[:, None] * freq[None, :]
        sign = jnp.where(dim < HEAD // 2, -1.0, 1.0)[None, :]
        out += [jnp.cos(angle), jnp.sin(angle) * sign]
    return out


def split_heads(
    inputs,
    norm_gain,
    wq_packed,
    wq_scales,
    key_weight,
    value_weight,
    wo_weight,
    key_cache,
    value_cache,
    lengths,
):
    nw, nh, nb = lax.axis_size("width"), lax.axis_size("hidden"), lax.axis_size("batch")
    swap = [(0, 1), (1, 0)]
    k_mate = lax.ppermute(key_cache, "batch", swap)
    v_mate = lax.ppermute(value_cache, "batch", swap)
    len_mate = lax.ppermute(lengths, "batch", swap)

    own, *sends = project(
        inputs, norm_gain, wq_packed, wq_scales, key_weight, value_weight, nw, nb
    )
    own, k_mate, v_mate, len_mate, *sends = lax.optimization_barrier(
        (own, k_mate, v_mate, len_mate, *sends)
    )
    first = lax.axis_index("batch") == 0
    len_all = jnp.where(
        first, jnp.concatenate([lengths, len_mate]), jnp.concatenate([len_mate, lengths])
    )
    positions = jnp.concatenate([len_all + step for step in range(STEPS)])
    table = rotary_tables(positions)
    parts = [
        lax.ppermute(piece, "width", [(i, i ^ s) for i in range(nw)])
        for s, piece in enumerate(sends, 1)
    ]
    heads = 2 * wq_packed.shape[1] // nb // HEAD
    depth = heads * HEAD
    early, middle, late = EARLY * depth // 8, MIDDLE * depth // 8, LATE * depth // 8
    w_early = fetch_weight(wo_weight, 0, early, depth, own)
    mixed, w_middle = attend(
        own, parts[::-1], table, len_all, key_cache, k_mate, value_cache, v_mate, wo_weight, early, middle,
        w_early, heads,
    )
    w_late = fetch_weight(wo_weight, early + middle, late, depth, mixed)
    pieces = [mixed] + [
        lax.ppermute(mixed, "width", [(i, i ^ s) for i in range(nw)]) for s in range(1, nw)
    ]
    here, across_core, across_chip, across_both = output(pieces, [w_early, w_middle, w_late])
    relay = lax.ppermute(across_both, "batch", swap)
    leaving = (across_chip + relay.astype(F32)).astype(BF16)
    leaving, across_core = lax.optimization_barrier((leaving, across_core))
    far = lax.ppermute(leaving, "hidden", swap)
    near = lax.ppermute(across_core, "batch", swap)
    sums = here + far.astype(F32) + near.astype(F32)
    return sums.astype(BF16)


def solution(mesh):
    sizes = mesh.shape

    def on_device(*args):
        kv_local = args[4].shape[1] // HEAD
        fits = (
            sizes["batch"] == 2
            and sizes["hidden"] == 2
            and kv_local == 2
            and sizes["width"] == sizes["hidden"] * sizes["batch"]
            and args[0].shape[1] // sizes["width"] == 2 * args[9].shape[0]
            and args[0].shape[2] % 512 == 0
            and STEPS * args[0].shape[1] // sizes["width"] % 8 == 0
        )
        return split_heads(*args) if fits else general(*args)

    in_specs = (
        P(None, "groups", "width"),
        P("width"),
        P("width", "hidden"),
        P("width", "hidden"),
        P("width", "hidden"),
        P("width", "hidden"),
        P("hidden", "width"),
        P(("groups", "width", "batch"), None, "hidden"),
        P(("groups", "width", "batch"), None, "hidden"),
        P(("groups", "width", "batch")),
    )
    out_specs = P(None, ("groups", "hidden", "batch"), "width")
    return jax.shard_map(
        on_device, mesh=mesh, in_specs=in_specs, out_specs=out_specs, check_vma=False
    )
```
